32 devices in a mesh: grp: 8 (over z, core), shard: 4 (over y, x).
Axes of the slice: x: 2, y: 2, z: 4, core: 2. Of those that a mesh axis runs over, the one named last changes fastest.
Arguments:
- gradient: bfloat16 [8, 4, 384, 1024], P('grp', None, 'shard'), may hold values from -300 to 300
- momentum: float32 [8, 4, 384, 1024], P('grp', None, 'shard'), may hold values from -6 to 6
- owner: int32 [8, 4, 1], P('grp'), may hold values from 0 to 3; in each aligned block of 4 rows (0 to 3, 4 to 7, ..., all dimensions but the last counted through in order) at most 2 rows name the same one
Outputs:
- update: bfloat16 [8, 4, 384, 1024], P('grp', None, 'shard')
- momentum_out: float32 [8, 4, 384, 1024], P('grp', None, 'shard')
- slot_rms: float32 [8, 4, 2], P('grp', 'shard')
The draws below stay inside these ranges and needn't reach their ends.
Inputs may be any that keep to these rules, and one draw needn't show every extreme that they name: `owner`: in every group no index of shard owns more than 2 matrices, and in some group some index owns exactly 2.
All inputs are finite; a program needn't handle non-finite values.
Results may differ from the reference program's by a relative error of at most 0.0085.
Values may be sent and summed in bfloat16 or wider, within the bound.
No kernel may reach another device: no remote copies, remote signals or barrier semaphores. Data moves between devices by JAX's collectives and lax.ppermute only.
A program may use at most 64 MiB of HBM per device.

```python
import math
import jax
import jax.numpy as jnp
import numpy as np
from jax import lax

ROWS = 384
COLS = 1024
ITERS = 3
MATS = 4
CAP = 2
GROUPS = 8
N_SHARD = 4


def draw_gradient(key, part):
    normal_base = jnp.clip(jax.random.normal(jax.random.fold_in(key, 11), (GROUPS, MATS, ROWS, COLS), jnp.float32), -5.0, 5.0)
    position = (jnp.arange(GROUPS)[:, None] * ROWS + jnp.arange(ROWS)[None, :]).astype(jnp.float32) / (GROUPS * ROWS)
    rising = (1.0 + 2.0 * position)[:, None, :, None]
    matrix_scale = jnp.exp(jax.random.uniform(jax.random.fold_in(key, 12), (GROUPS, MATS, 1, 1), jnp.float32, math.log(0.5), math.log(2.0)))
    block_level = jnp.exp(jax.random.uniform(jax.random.fold_in(key, 15), (N_SHARD,), jnp.float32, math.log(0.2), math.log(5.0)))
    block_scale = jnp.repeat(block_level, ROWS // N_SHARD)[None, None, :, None]
    values = normal_base * rising * matrix_scale * block_scale
    return values.astype(jnp.bfloat16)


def block_levels(own_key, shape, cuts, smallest, largest):
    gain, own = 1.0, jax.random.fold_in(own_key, 6)
    for axis_at, parts in cuts:
        draws = jnp.exp(jax.random.uniform(jax.random.fold_in(own, axis_at), (parts,), jnp.float32, smallest / len(cuts), largest / len(cuts)))
        gain = gain * jnp.repeat(draws, shape[axis_at] // parts).reshape([-1 if axis == axis_at else 1 for axis in range(len(shape))])
    return gain


def shared_out(key, own, number, rows, count, top, limit, skew):
    sequence = jax.random.permutation(key, count)
    crowded, common = portions_of(count, rows * top, limit, skew, True), portions_of(count, rows * top, limit, skew, False)
    places = jnp.arange(count)

    def named(sizes, rotation):
        used = int((sizes > 0).sum())
        fixed = max(1, used // 4)
        moved = fixed + (places - fixed + rotation * (used - fixed)) % max(1, count - fixed)
        return jnp.zeros((count,), jnp.int32).at[sequence[jnp.where(places < fixed, places, moved)]].set(jnp.asarray(sizes, jnp.int32))

    sizes = jnp.where(number % 4 == 0, named(crowded, number // 4), named(common, number - number // 4 - 1))
    mixed = jax.random.permutation(jax.random.fold_in(own, 3), count)
    source_of, receiver = mixed[0:count // 2 * 2:2], mixed[1:count // 2 * 2:2]
    room = jnp.minimum(sizes[source_of] - 1, limit - sizes[receiver]) // 2
    room = jnp.where((source_of == sequence[0]) | (receiver == sequence[0]) | (sizes[receiver] == 0), 0, jnp.maximum(room, 0))
    moved = jax.random.randint(jax.random.fold_in(own, 4), (count // 2,), 0, 1 << 20) % (room + 1)
    sizes = sizes.at[source_of].add(-moved).at[receiver].add(moved)
    labels = jnp.searchsorted(jnp.cumsum(sizes), jnp.arange(rows * top), side="right").astype(jnp.int32)
    table = labels.reshape(top, rows).T
    table = table[jax.random.permutation(jax.random.fold_in(own, 1), rows)]
    rotation = jax.random.randint(jax.random.fold_in(own, 2), (rows, 1), 0, top)
    return jnp.take_along_axis(table, (jnp.arange(top)[None, :] + rotation) % top, axis=1)


def portions_of(number_of, total, reach, slope, full):
    portions = [(1 << 20) // math.isqrt(grade ** slope) + 1 for grade in range(1, number_of + 1)]
    largest = reach if full else min(reach, max(-(-total // number_of), total * portions[0] // sum(portions)))
    least = 1 if total - largest >= number_of - 1 else 0
    given, rest = [largest] + [least] * (number_of - 1), total - largest - least * (number_of - 1)
    while rest > 0:
        candidates = [i for i in range(1, number_of) if given[i] < largest] or [i for i in range(1, number_of) if given[i] < reach]
        mass, remaining = sum([portions[i] for i in candidates]), rest
        for i in candidates:
            addition = min(reach - given[i], max(1, remaining * portions[i] // mass), rest)
            given[i] = given[i] + addition
            rest = rest - addition
    return np.array(given)


def centred(own_key, dims, scale, most, split=(), kind=jnp.bfloat16):
    gain = block_levels(own_key, dims, split, -0.22, 0.18) if split else 1.0
    result = jax.random.normal(own_key, dims, jnp.float32) * scale * gain
    return jnp.minimum(jnp.maximum(result, -most), most).astype(kind)


def setup_inputs(seed: int = 0) -> dict:
    key_list = jax.random.split(jax.random.key(seed), 4)
    gradient = draw_gradient(jax.random.fold_in(key_list[3], 71), 0)
    momentum = centred(key_list[1], (GROUPS, MATS, ROWS, COLS), 1.0, 6.0, ((0, 8), (2, 4)), jnp.float32)
    owner_keys = jax.random.split(jax.random.fold_in(key_list[2], 1), GROUPS * MATS // MATS)
    owner_turns = jax.random.permutation(jax.random.fold_in(key_list[2], 3), GROUPS * MATS // MATS)
    owner = jax.vmap(lambda own, number: shared_out(jax.random.fold_in(key_list[2], 2), own, number, MATS, N_SHARD, 1, CAP, 2))(owner_keys, owner_turns).reshape((GROUPS, MATS, 1))
    return dict(gradient=gradient, momentum=momentum, owner=owner)


QUINTIC_A = 3.4445
QUINTIC_B = -4.775
QUINTIC_C = 2.0315
MOMENTUM_DECAY = 0.95
CLIP_LEVEL = 0.5

def newton(matrix):
    wide = matrix.astype(jnp.float32)
    square_sum = jnp.sum(wide * wide)
    iterate = (wide / (jnp.sqrt(square_sum) + 1e-07)).astype(jnp.bfloat16)
    for repeat in range(ITERS):
        gram_matrix = jnp.dot(iterate, iterate.T, preferred_element_type=jnp.float32).astype(jnp.bfloat16)
        squared = jnp.dot(gram_matrix, gram_matrix, preferred_element_type=jnp.float32)
        blended = (QUINTIC_B * gram_matrix.astype(jnp.float32) + QUINTIC_C * squared).astype(jnp.bfloat16)
        iterate = (QUINTIC_A * iterate.astype(jnp.float32) + jnp.dot(blended, iterate, preferred_element_type=jnp.float32)).astype(jnp.bfloat16)
    return (iterate, square_sum)

def reference(gradient, momentum, owner):
    grad_wide = gradient.astype(jnp.float32)
    mean_square = jnp.sum(grad_wide * grad_wide) / (GROUPS * MATS * ROWS * COLS)
    clip_factor = jnp.minimum(jnp.float32(1.0), CLIP_LEVEL / jnp.sqrt(mean_square + 1e-06))
    momentum_out = MOMENTUM_DECAY * momentum + clip_factor * grad_wide
    nesterov = (clip_factor * grad_wide + MOMENTUM_DECAY * momentum_out).astype(jnp.bfloat16)
    stacked = nesterov.reshape(GROUPS * MATS, ROWS, COLS)
    ortho, squares = lax.map(newton, stacked)
    update = (ortho.astype(jnp.float32) * math.sqrt(COLS)).astype(jnp.bfloat16).reshape(GROUPS, MATS, ROWS, COLS)
    owners = owner[:, :, 0]
    owner_hot = (owners[:, :, None] == jnp.arange(N_SHARD, dtype=jnp.int32)[None, None, :]).astype(jnp.int32)
    ranking = lax.optimization_barrier(jnp.sum((jnp.cumsum(owner_hot, axis=1) - owner_hot) * owner_hot, axis=2))
    slot_hot = (ranking[:, :, None] == jnp.arange(CAP, dtype=jnp.int32)[None, None, :]).astype(jnp.float32)
    matrix_rms = jnp.sqrt(squares.reshape(GROUPS, MATS)) / math.sqrt(ROWS * COLS)
    slot_rms = lax.optimization_barrier(jnp.sum(owner_hot.astype(jnp.float32)[:, :, :, None] * slot_hot[:, :, None, :] * matrix_rms[:, :, None, None], axis=1))
    return (update, momentum_out, slot_rms)
```

```python
import functools
import math

import jax
import jax.numpy as jnp
from jax import lax
from jax.experimental import pallas as pl
from jax.experimental.pallas import tpu as pltpu
from jax.sharding import PartitionSpec as P

ITERS = 3
CAP = 2
LANES = 128
CHUNK = 24

QUINTIC_A = 3.4445
QUINTIC_B = -4.775
QUINTIC_C = 2.0315
MOMENTUM_DECAY = 0.95
CLIP_LEVEL = 0.5


VMEM = pl.BlockSpec(memory_space=pltpu.VMEM)
SMEM = pl.BlockSpec(memory_space=pltpu.SMEM)
ANY = pl.BlockSpec(memory_space=pl.ANY)


def partner(me, step, shards):
    if shards & (shards - 1) == 0:
        return me ^ step
    return lax.rem(me + step, shards)


def source(me, step, shards):
    if shards & (shards - 1) == 0:
        return me ^ step
    return lax.rem(me + shards - step, shards)


def pack_kernel(shards, me_ref, grad_hbm, mom_hbm, sums_ref, *rest):
    payloads, (grad_buf, mom_buf, grad_sem, mom_sem) = rest[:shards], rest[shards:]
    rows = grad_hbm.shape[1]
    copies = []
    for step in range(shards):
        target = partner(me_ref[0], step, shards)
        for hbm, buf, sem in ((grad_hbm, grad_buf, grad_sem), (mom_hbm, mom_buf, mom_sem)):
            copy = pltpu.make_async_copy(hbm.at[target], buf.at[step], sem.at[step])
            copy.start()
            copies.append(copy)
    lane = lax.broadcasted_iota(jnp.int32, (1, sums_ref.shape[1]), 1)
    sums = jnp.zeros((1, sums_ref.shape[1]), jnp.float32)
    order = list(range(1, shards)) + [0]
    for step in order:
        copies[2 * step].wait()
        copies[2 * step + 1].wait()
        gg = gm = mm = None
        for at in range(0, rows, CHUNK):
            part = pl.ds(at, CHUNK)
            grad_narrow = grad_buf[step, part]
            mom = mom_buf[step, part]
            payloads[step][part] = grad_narrow
            payloads[step][pl.ds(rows + at, CHUNK)] = mom.astype(jnp.bfloat16)
            grad = grad_narrow.astype(jnp.float32)
            a, b, c = (jnp.sum(p, axis=0, keepdims=True) for p in (grad * grad, grad * mom, mom * mom))
            gg, gm, mm = (a, b, c) if gg is None else (gg + a, gm + b, mm + c)
        matrix = partner(me_ref[0], step, shards)
        for kind, value in enumerate((gg, gm, mm)):
            total = jnp.sum(value, axis=1, keepdims=True)
            sums = jnp.where(lane == matrix + kind * shards, total, sums)
    sums_ref[...] = jnp.broadcast_to(sums, sums_ref.shape)


def clip_of(sums, matrices, element_count):
    lane = lax.broadcasted_iota(jnp.int32, sums.shape, 1)
    total = jnp.sum(jnp.where(lane < matrices, sums, 0.0))
    mean_square = jnp.full((1, LANES), total, jnp.float32) / element_count
    return jnp.minimum(jnp.float32(1.0), CLIP_LEVEL / jnp.sqrt(mean_square + 1e-06))


def newton_kernel(shards, element_count, me_ref, sums_ref, *rest):
    blocks, (out_ref, clip_ref, iterate) = rest[:shards], rest[shards:]
    rows, columns = out_ref.shape[1:]
    clip = clip_of(sums_ref[...], shards, element_count)
    clip_ref[...] = clip
    clip = clip[0, 0]
    squares = jnp.zeros((1, columns), jnp.float32)
    for step in range(shards):
        for at in range(0, rows, CHUNK):
            grad = clip * blocks[step][pl.ds(at, CHUNK)].astype(jnp.float32)
            out = MOMENTUM_DECAY * blocks[step][pl.ds(rows + at, CHUNK)].astype(jnp.float32) + grad
            nesterov = (grad + MOMENTUM_DECAY * out).astype(jnp.bfloat16)
            iterate[pl.ds(step * rows + at, CHUNK)] = nesterov
            wide = nesterov.astype(jnp.float32)
            squares = squares + jnp.sum(wide * wide, axis=0, keepdims=True)
    norm = jnp.sqrt(jnp.full((1, 1), jnp.sum(squares), jnp.float32)) + 1e-07
    scale = (1.0 / norm)[0, 0]
    iterate[...] = (iterate[...].astype(jnp.float32) * scale).astype(jnp.bfloat16)
    for repeat in range(ITERS):
        x = iterate[...]
        gram = lax.dot_general(
            x, x, (((1,), (1,)), ((), ())), preferred_element_type=jnp.float32
        ).astype(jnp.bfloat16)
        squared = jnp.dot(gram, gram, preferred_element_type=jnp.float32)
        blended = (QUINTIC_B * gram.astype(jnp.float32) + QUINTIC_C * squared).astype(jnp.bfloat16)
        product = jnp.dot(blended, x, preferred_element_type=jnp.float32)
        iterate[...] = (QUINTIC_A * x.astype(jnp.float32) + product).astype(jnp.bfloat16)
    for step in range(shards):
        target = partner(me_ref[0], step, shards) if step else me_ref[0]
        if shards & (shards - 1):
            target = source(me_ref[0], step, shards)
        x = iterate[pl.ds(step * rows, rows)]
        out_ref[target] = (x.astype(jnp.float32) * math.sqrt(columns)).astype(jnp.bfloat16)


def momentum_kernel(shards, place_ref, owner_ref, clip_ref, sums_ref, grad_ref, mom_ref, out_ref, slot_ref):
    rows, columns = grad_ref.shape[1:]
    clip = clip_ref[0, 0]
    out_ref[...] = MOMENTUM_DECAY * mom_ref[...] + clip * grad_ref[...].astype(jnp.float32)

    @pl.when(pl.program_id(0) == 0)
    def _():
        me, group = place_ref[0], place_ref[1]
        row = lax.broadcasted_iota(jnp.int32, sums_ref.shape, 0)
        inside = (row >= group * shards) & (row < (group + 1) * shards)
        sums = jnp.sum(jnp.where(inside, sums_ref[...], 0.0), axis=0, keepdims=True)
        lane = lax.broadcasted_iota(jnp.int32, sums.shape, 1)
        grad_part = clip * (1.0 + MOMENTUM_DECAY)
        mom_part = MOMENTUM_DECAY * MOMENTUM_DECAY
        slots = [jnp.float32(0.0)] * CAP
        count = jnp.int32(0)
        for matrix in range(shards):
            gg, gm, mm = (
                jnp.sum(jnp.where(lane == matrix + kind * shards, sums, 0.0)) for kind in range(3)
            )
            square = grad_part * grad_part * gg + 2.0 * grad_part * mom_part * gm + mom_part * mom_part * mm
            hit = owner_ref[matrix] == me
            for slot in range(CAP):
                slots[slot] = slots[slot] + jnp.where(hit & (count == slot), square, 0.0)
            count = count + hit.astype(jnp.int32)
        lane = lax.broadcasted_iota(jnp.int32, (1, CAP), 1)
        out = jnp.zeros((1, CAP), jnp.float32)
        for slot in range(CAP):
            out = jnp.where(lane == slot, slots[slot], out)
        slot_ref[...] = (jnp.sqrt(jnp.maximum(out, 0.0)) / math.sqrt(shards * rows * columns)).reshape(1, 1, CAP)


def body(gradient, momentum, owner):
    shards = lax.axis_size("shard")
    devices = shards * lax.axis_size("grp")
    matrices, rows, columns = gradient.shape[1:]
    assert matrices == shards
    element_count = matrices * rows * columns * devices
    width = -(-3 * matrices // LANES) * LANES
    me = lax.axis_index("shard").astype(jnp.int32)
    group = lax.axis_index("grp").astype(jnp.int32)
    grad, mom = gradient[0], momentum[0]
    block = jax.ShapeDtypeStruct((2 * rows, columns), jnp.bfloat16)
    table = jax.ShapeDtypeStruct((devices, width), jnp.float32)
    sums, *payloads = pl.pallas_call(
        functools.partial(pack_kernel, shards),
        name="pack",
        out_shape=[table] + [block] * shards,
        in_specs=[SMEM, ANY, ANY],
        out_specs=[VMEM] * (1 + shards),
        scratch_shapes=[
            pltpu.VMEM((shards, rows, columns), jnp.bfloat16),
            pltpu.VMEM((shards, rows, columns), jnp.float32),
            pltpu.SemaphoreType.DMA((shards,)),
            pltpu.SemaphoreType.DMA((shards,)),
        ],
        compiler_params=pltpu.CompilerParams(vmem_limit_bytes=12 * 2**20),
        cost_estimate=pl.CostEstimate(flops=10 * grad.size, bytes_accessed=10 * grad.size, transcendentals=0),
    )(me[None], grad, mom)
    blocks = [payloads[0]]
    for step in range(1, shards):
        pairs = [(i, (i ^ step) if shards & (shards - 1) == 0 else (i + step) % shards) for i in range(shards)]
        blocks.append(lax.ppermute(payloads[step], "shard", pairs))
    sums = lax.all_to_all(sums, ("grp", "shard"), 0, 0, tiled=True)
    scaled, clip = pl.pallas_call(
        functools.partial(newton_kernel, shards, element_count),
        name="newton",
        out_shape=[
            jax.ShapeDtypeStruct((shards, rows, columns), jnp.bfloat16),
            jax.ShapeDtypeStruct((1, LANES), jnp.float32),
        ],
        in_specs=[SMEM] + [VMEM] * (1 + shards),
        out_specs=[VMEM, VMEM],
        scratch_shapes=[pltpu.VMEM((shards * rows, columns), jnp.bfloat16)],
        compiler_params=pltpu.CompilerParams(vmem_limit_bytes=16 * 2**20),
        cost_estimate=pl.CostEstimate(flops=4_000_000_000, bytes_accessed=8 * grad.size, transcendentals=0),
    )(me[None], sums, *blocks)
    update = lax.all_to_all(scaled, "shard", 0, 0, tiled=True)[None]
    momentum_out, slot_rms = pl.pallas_call(
        functools.partial(momentum_kernel, shards),
        name="momentum",
        grid=(matrices,),
        out_shape=[
            jax.ShapeDtypeStruct(mom.shape, jnp.float32),
            jax.ShapeDtypeStruct((1, 1, CAP), jnp.float32),
        ],
        in_specs=[
            SMEM,
            SMEM,
            pl.BlockSpec((1, LANES), lambda i: (0, 0)),
            pl.BlockSpec((devices, width), lambda i: (0, 0)),
            pl.BlockSpec((1, rows, columns), lambda i: (i, 0, 0)),
            pl.BlockSpec((1, rows, columns), lambda i: (i, 0, 0)),
        ],
        out_specs=[
            pl.BlockSpec((1, rows, columns), lambda i: (i, 0, 0)),
            pl.BlockSpec((1, 1, CAP), lambda i: (0, 0, 0)),
        ],
        compiler_params=pltpu.CompilerParams(vmem_limit_bytes=8 * 2**20),
        cost_estimate=pl.CostEstimate(flops=4 * grad.size, bytes_accessed=10 * grad.size, transcendentals=0),
    )(jnp.stack([me, group]), owner[0, :, 0], clip, sums, grad, mom)
    return (update, momentum_out[None], slot_rms)


def solution(mesh):
    return jax.shard_map(
        body,
        mesh=mesh,
        in_specs=(
            P("grp", None, "shard", None),
            P("grp", None, "shard", None),
            P("grp", None, None),
        ),
        out_specs=(
            P("grp", None, "shard", None),
            P("grp", None, "shard", None),
            P("grp", "shard", None),
        ),
        check_vma=False,
    )
```

```python
import functools
import math

import jax
import jax.numpy as jnp
from jax import lax
from jax.experimental import pallas as pl
from jax.experimental.pallas import tpu as pltpu
from jax.sharding import PartitionSpec as P

ITERS = 3
CAP = 2
LANES = 128
CHUNK = 24

QUINTIC_A = 3.4445
QUINTIC_B = -4.775
QUINTIC_C = 2.0315
MOMENTUM_DECAY = 0.95
CLIP_LEVEL = 0.5


VMEM = pl.BlockSpec(memory_space=pltpu.VMEM)
SMEM = pl.BlockSpec(memory_space=pltpu.SMEM)
ANY = pl.BlockSpec(memory_space=pl.ANY)


def partner(me, step, shards):
    if shards & (shards - 1) == 0:
        return me ^ step
    return lax.rem(me + step, shards)


def source(me, step, shards):
    if shards & (shards - 1) == 0:
        return me ^ step
    return lax.rem(me + shards - step, shards)


def pack_kernel(shards, me_ref, grad_hbm, mom_hbm, sums_ref, *rest):
    payloads, (grad_buf, mom_buf, grad_sem, mom_sem) = rest[:shards], rest[shards:]
    rows = grad_hbm.shape[1]
    copies = []
    for step in range(shards):
        target = partner(me_ref[0], step, shards)
        for hbm, buf, sem in ((grad_hbm, grad_buf, grad_sem), (mom_hbm, mom_buf, mom_sem)):
            copy = pltpu.make_async_copy(hbm.at[target], buf.at[step], sem.at[step])
            copy.start()
            copies.append(copy)
    lane = lax.broadcasted_iota(jnp.int32, (1, sums_ref.shape[1]), 1)
    sums = jnp.zeros((1, sums_ref.shape[1]), jnp.float32)
    order = list(range(1, shards)) + [0]
    for step in order:
        copies[2 * step].wait()
        copies[2 * step + 1].wait()
        gg = gm = mm = None
        for at in range(0, rows, CHUNK):
            part = pl.ds(at, CHUNK)
            grad_narrow = grad_buf[step, part]
            mom = mom_buf[step, part]
            payloads[step][part] = grad_narrow
            payloads[step][pl.ds(rows + at, CHUNK)] = mom.astype(jnp.bfloat16)
            grad = grad_narrow.astype(jnp.float32)
            a, b, c = (jnp.sum(p, axis=0, keepdims=True) for p in (grad * grad, grad * mom, mom * mom))
            gg, gm, mm = (a, b, c) if gg is None else (gg + a, gm + b, mm + c)
        matrix = partner(me_ref[0], step, shards)
        for kind, value in enumerate((gg, gm, mm)):
            total = jnp.sum(value, axis=1, keepdims=True)
            sums = jnp.where(lane == matrix + kind * shards, total, sums)
    sums_ref[...] = jnp.broadcast_to(sums, sums_ref.shape)


def clip_of(sums, matrices, element_count):
    lane = lax.broadcasted_iota(jnp.int32, sums.shape, 1)
    total = jnp.sum(jnp.where(lane < matrices, sums, 0.0))
    mean_square = jnp.full((1, LANES), total, jnp.float32) / element_count
    return jnp.minimum(jnp.float32(1.0), CLIP_LEVEL / jnp.sqrt(mean_square + 1e-06))


def newton_kernel(shards, element_count, me_ref, sums_ref, *rest):
    blocks, (out_ref, clip_ref, iterate) = rest[:shards], rest[shards:]
    rows, columns = out_ref.shape[1:]
    clip = clip_of(sums_ref[...], shards, element_count)
    clip_ref[...] = clip
    clip = clip[0, 0]
    squares = jnp.zeros((1, columns), jnp.float32)
    for step in range(shards):
        for at in range(0, rows, CHUNK):
            grad = clip * blocks[step][pl.ds(at, CHUNK)].astype(jnp.float32)
            out = MOMENTUM_DECAY * blocks[step][pl.ds(rows + at, CHUNK)].astype(jnp.float32) + grad
            nesterov = (grad + MOMENTUM_DECAY * out).astype(jnp.bfloat16)
            iterate[pl.ds(step * rows + at, CHUNK)] = nesterov
            wide = nesterov.astype(jnp.float32)
            squares = squares + jnp.sum(wide * wide, axis=0, keepdims=True)
    norm = jnp.sqrt(jnp.full((1, 1), jnp.sum(squares), jnp.float32)) + 1e-07
    scale = (1.0 / norm)[0, 0]
    iterate[...] = (iterate[...].astype(jnp.float32) * scale).astype(jnp.bfloat16)
    for repeat in range(ITERS):
        x = iterate[...]
        gram = lax.dot_general(
            x, x, (((1,), (1,)), ((), ())), preferred_element_type=jnp.float32
        ).astype(jnp.bfloat16)
        squared = jnp.dot(gram, gram, preferred_element_type=jnp.float32)
        blended = (QUINTIC_B * gram.astype(jnp.float32) + QUINTIC_C * squared).astype(jnp.bfloat16)
        product = jnp.dot(blended, x, preferred_element_type=jnp.float32)
        iterate[...] = (QUINTIC_A * x.astype(jnp.float32) + product).astype(jnp.bfloat16)
    for step in range(shards):
        target = partner(me_ref[0], step, shards) if step else me_ref[0]
        if shards & (shards - 1):
            target = source(me_ref[0], step, shards)
        x = iterate[pl.ds(step * rows, rows)]
        out_ref[target] = (x.astype(jnp.float32) * math.sqrt(columns)).astype(jnp.bfloat16)


def momentum_kernel(shards, place_ref, owner_ref, clip_ref, sums_ref, grad_ref, mom_ref, out_ref, slot_ref):
    rows, columns = grad_ref.shape[1:]
    clip = clip_ref[0, 0]
    out_ref[...] = MOMENTUM_DECAY * mom_ref[...] + clip * grad_ref[...].astype(jnp.float32)

    @pl.when(pl.program_id(0) == 0)
    def _():
        me, group = place_ref[0], place_ref[1]
        row = lax.broadcasted_iota(jnp.int32, sums_ref.shape, 0)
        inside = (row >= group * shards) & (row < (group + 1) * shards)
        sums = jnp.sum(jnp.where(inside, sums_ref[...], 0.0), axis=0, keepdims=True)
        lane = lax.broadcasted_iota(jnp.int32, sums.shape, 1)
        grad_part = clip * (1.0 + MOMENTUM_DECAY)
        mom_part = MOMENTUM_DECAY * MOMENTUM_DECAY
        slots = [jnp.float32(0.0)] * CAP
        count = jnp.int32(0)
        for matrix in range(shards):
            gg, gm, mm = (
                jnp.sum(jnp.where(lane == matrix + kind * shards, sums, 0.0)) for kind in range(3)
            )
            square = grad_part * grad_part * gg + 2.0 * grad_part * mom_part * gm + mom_part * mom_part * mm
            hit = owner_ref[matrix] == me
            for slot in range(CAP):
                slots[slot] = slots[slot] + jnp.where(hit & (count == slot), square, 0.0)
            count = count + hit.astype(jnp.int32)
        lane = lax.broadcasted_iota(jnp.int32, (1, CAP), 1)
        out = jnp.zeros((1, CAP), jnp.float32)
        for slot in range(CAP):
            out = jnp.where(lane == slot, slots[slot], out)
        slot_ref[...] = (jnp.sqrt(jnp.maximum(out, 0.0)) / math.sqrt(shards * rows * columns)).reshape(1, 1, CAP)


def body(gradient, momentum, owner):
    shards = lax.axis_size("shard")
    devices = shards * lax.axis_size("grp")
    matrices, rows, columns = gradient.shape[1:]
    assert matrices == shards
    element_count = matrices * rows * columns * devices
    width = -(-3 * matrices // LANES) * LANES
    me = lax.axis_index("shard").astype(jnp.int32)
    group = lax.axis_index("grp").astype(jnp.int32)
    grad, mom = gradient[0], momentum[0]
    block = jax.ShapeDtypeStruct((2 * rows, columns), jnp.bfloat16)
    table = jax.ShapeDtypeStruct((devices, width), jnp.float32)
    sums, *payloads = pl.pallas_call(
        functools.partial(pack_kernel, shards),
        name="pack",
        out_shape=[table] + [block] * shards,
        in_specs=[SMEM, ANY, ANY],
        out_specs=[VMEM] * (1 + shards),
        scratch_shapes=[
            pltpu.VMEM((shards, rows, columns), jnp.bfloat16),
            pltpu.VMEM((shards, rows, columns), jnp.float32),
            pltpu.SemaphoreType.DMA((shards,)),
            pltpu.SemaphoreType.DMA((shards,)),
        ],
        compiler_params=pltpu.CompilerParams(vmem_limit_bytes=52 * 2**20),
        cost_estimate=pl.CostEstimate(flops=10 * grad.size, bytes_accessed=10 * grad.size, transcendentals=0),
    )(me[None], grad, mom)
    blocks = [payloads[0]]
    for step in range(1, shards):
        pairs = [(i, (i ^ step) if shards & (shards - 1) == 0 else (i + step) % shards) for i in range(shards)]
        blocks.append(lax.ppermute(payloads[step], "shard", pairs))
    sums = lax.all_to_all(sums, ("grp", "shard"), 0, 0, tiled=True)
    scaled, clip = pl.pallas_call(
        functools.partial(newton_kernel, shards, element_count),
        name="newton",
        out_shape=[
            jax.ShapeDtypeStruct((shards, rows, columns), jnp.bfloat16),
            jax.ShapeDtypeStruct((1, LANES), jnp.float32),
        ],
        in_specs=[SMEM] + [VMEM] * (1 + shards),
        out_specs=[VMEM, VMEM],
        scratch_shapes=[pltpu.VMEM((shards * rows, columns), jnp.bfloat16)],
        compiler_params=pltpu.CompilerParams(vmem_limit_bytes=16 * 2**20),
        cost_estimate=pl.CostEstimate(flops=4_000_000_000, bytes_accessed=8 * grad.size, transcendentals=0),
    )(me[None], sums, *blocks)
    update = lax.all_to_all(scaled, "shard", 0, 0, tiled=True)[None]
    momentum_out, slot_rms = pl.pallas_call(
        functools.partial(momentum_kernel, shards),
        name="momentum",
        grid=(matrices,),
        out_shape=[
            jax.ShapeDtypeStruct(mom.shape, jnp.float32),
            jax.ShapeDtypeStruct((1, 1, CAP), jnp.float32),
        ],
        in_specs=[
            SMEM,
            SMEM,
            pl.BlockSpec((1, LANES), lambda i: (0, 0)),
            pl.BlockSpec((devices, width), lambda i: (0, 0)),
            pl.BlockSpec((1, rows, columns), lambda i: (i, 0, 0)),
            pl.BlockSpec((1, rows, columns), lambda i: (i, 0, 0)),
        ],
        out_specs=[
            pl.BlockSpec((1, rows, columns), lambda i: (i, 0, 0)),
            pl.BlockSpec((1, 1, CAP), lambda i: (0, 0, 0)),
        ],
        compiler_params=pltpu.CompilerParams(vmem_limit_bytes=8 * 2**20),
        cost_estimate=pl.CostEstimate(flops=4 * grad.size, bytes_accessed=10 * grad.size, transcendentals=0),
    )(jnp.stack([me, group]), owner[0, :, 0], clip, sums, grad, mom)
    return (update, momentum_out[None], slot_rms)


def solution(mesh):
    return jax.shard_map(
        body,
        mesh=mesh,
        in_specs=(
            P("grp", None, "shard", None),
            P("grp", None, "shard", None),
            P("grp", None, None),
        ),
        out_specs=(
            P("grp", None, "shard", None),
            P("grp", None, "shard", None),
            P("grp", "shard", None),
        ),
        check_vma=False,
    )
```

```python
import functools
import math

import jax
import jax.numpy as jnp
from jax import lax
from jax.experimental import pallas as pl
from jax.experimental.pallas import tpu as pltpu
from jax.sharding import PartitionSpec as P

ITERS = 3
CAP = 2
LANES = 128
CHUNK = 24

QUINTIC_A = 3.4445
QUINTIC_B = -4.775
QUINTIC_C = 2.0315
MOMENTUM_DECAY = 0.95
CLIP_LEVEL = 0.5


VMEM = pl.BlockSpec(memory_space=pltpu.VMEM)
SMEM = pl.BlockSpec(memory_space=pltpu.SMEM)
ANY = pl.BlockSpec(memory_space=pl.ANY)


def partner(me, step, shards):
    if shards & (shards - 1) == 0:
        return me ^ step
    return (me + step) % shards


def exchange(block, step, shards, back=False):
    pairs = [(i, partner(i, step, shards)) for i in range(shards)]
    return lax.ppermute(block, "shard", [(b, a) if back else (a, b) for a, b in pairs])


def pack_kernel(shards, me_ref, grad_hbm, mom_hbm, sums_ref, *rest):
    payloads, (grad_buf, mom_buf, grad_sem, mom_sem) = rest[:shards], rest[shards:]
    rows = grad_hbm.shape[1]
    copies = []
    for step in range(shards):
        target = partner(me_ref[0], step, shards)
        for hbm, buf, sem in ((grad_hbm, grad_buf, grad_sem), (mom_hbm, mom_buf, mom_sem)):
            copy = pltpu.make_async_copy(hbm.at[target], buf.at[step], sem.at[step])
            copy.start()
            copies.append(copy)
    lane = lax.broadcasted_iota(jnp.int32, (1, sums_ref.shape[1]), 1)
    sums = jnp.zeros((1, sums_ref.shape[1]), jnp.float32)
    order = list(range(1, shards)) + [0]
    for step in order:
        copies[2 * step].wait()
        copies[2 * step + 1].wait()
        gg = gm = mm = None
        for at in range(0, rows, CHUNK):
            part = pl.ds(at, CHUNK)
            grad_narrow = grad_buf[step, part]
            mom = mom_buf[step, part]
            payloads[step][part] = grad_narrow
            payloads[step][pl.ds(rows + at, CHUNK)] = mom.astype(jnp.bfloat16)
            grad = grad_narrow.astype(jnp.float32)
            a, b, c = (jnp.sum(p, axis=0, keepdims=True) for p in (grad * grad, grad * mom, mom * mom))
            gg, gm, mm = (a, b, c) if gg is None else (gg + a, gm + b, mm + c)
        matrix = partner(me_ref[0], step, shards)
        for kind, value in enumerate((gg, gm, mm)):
            total = jnp.sum(value, axis=1, keepdims=True)
            sums = jnp.where(lane == matrix + kind * shards, total, sums)
    sums_ref[...] = jnp.broadcast_to(sums, sums_ref.shape)


def clip_of(sums, matrices, element_count):
    lane = lax.broadcasted_iota(jnp.int32, sums.shape, 1)
    total = jnp.sum(jnp.where(lane < matrices, sums, 0.0))
    mean_square = jnp.full((1, LANES), total, jnp.float32) / element_count
    return jnp.minimum(jnp.float32(1.0), CLIP_LEVEL / jnp.sqrt(mean_square + 1e-06))


def newton_kernel(shards, element_count, sums_ref, *rest):
    blocks, outs, (clip_ref, iterate) = rest[:shards], rest[shards : 2 * shards], rest[2 * shards :]
    rows, columns = outs[0].shape
    clip = clip_of(sums_ref[...], shards, element_count)
    clip_ref[...] = clip
    clip = clip[0, 0]
    squares = jnp.zeros((1, columns), jnp.float32)
    for step in range(shards):
        for at in range(0, rows, CHUNK):
            grad = clip * blocks[step][pl.ds(at, CHUNK)].astype(jnp.float32)
            out = MOMENTUM_DECAY * blocks[step][pl.ds(rows + at, CHUNK)].astype(jnp.float32) + grad
            nesterov = (grad + MOMENTUM_DECAY * out).astype(jnp.bfloat16)
            iterate[pl.ds(step * rows + at, CHUNK)] = nesterov
            wide = nesterov.astype(jnp.float32)
            squares = squares + jnp.sum(wide * wide, axis=0, keepdims=True)
    norm = jnp.sqrt(jnp.full((1, 1), jnp.sum(squares), jnp.float32)) + 1e-07
    scale = (1.0 / norm)[0, 0]
    iterate[...] = (iterate[...].astype(jnp.float32) * scale).astype(jnp.bfloat16)
    for repeat in range(ITERS):
        x = iterate[...]
        gram = lax.dot_general(
            x, x, (((1,), (1,)), ((), ())), preferred_element_type=jnp.float32
        ).astype(jnp.bfloat16)
        squared = jnp.dot(gram, gram, preferred_element_type=jnp.float32)
        blended = (QUINTIC_B * gram.astype(jnp.float32) + QUINTIC_C * squared).astype(jnp.bfloat16)
        product = jnp.dot(blended, x, preferred_element_type=jnp.float32)
        iterate[...] = (QUINTIC_A * x.astype(jnp.float32) + product).astype(jnp.bfloat16)
    for step in range(shards):
        x = iterate[pl.ds(step * rows, rows)]
        outs[step][...] = (x.astype(jnp.float32) * math.sqrt(columns)).astype(jnp.bfloat16)


def place_kernel(shards, me_ref, *rest):
    blocks, (out_hbm, sem) = rest[:shards], rest[shards:]
    copies = []
    for step in range(shards):
        target = partner(me_ref[0], step, shards)
        copy = pltpu.make_async_copy(blocks[step], out_hbm.at[target], sem.at[step])
        copy.start()
        copies.append(copy)
    for copy in copies:
        copy.wait()


def momentum_kernel(shards, place_ref, owner_ref, clip_ref, sums_ref, grad_ref, mom_ref, out_ref, slot_ref):
    rows, columns = grad_ref.shape[1:]
    clip = clip_ref[0, 0]
    out_ref[...] = MOMENTUM_DECAY * mom_ref[...] + clip * grad_ref[...].astype(jnp.float32)

    @pl.when(pl.program_id(0) == 0)
    def _():
        me, group = place_ref[0], place_ref[1]
        row = lax.broadcasted_iota(jnp.int32, sums_ref.shape, 0)
        inside = (row >= group * shards) & (row < (group + 1) * shards)
        sums = jnp.sum(jnp.where(inside, sums_ref[...], 0.0), axis=0, keepdims=True)
        lane = lax.broadcasted_iota(jnp.int32, sums.shape, 1)
        grad_part = clip * (1.0 + MOMENTUM_DECAY)
        mom_part = MOMENTUM_DECAY * MOMENTUM_DECAY
        slots = [jnp.float32(0.0)] * CAP
        count = jnp.int32(0)
        for matrix in range(shards):
            gg, gm, mm = (
                jnp.sum(jnp.where(lane == matrix + kind * shards, sums, 0.0)) for kind in range(3)
            )
            square = grad_part * grad_part * gg + 2.0 * grad_part * mom_part * gm + mom_part * mom_part * mm
            hit = owner_ref[matrix] == me
            for slot in range(CAP):
                slots[slot] = slots[slot] + jnp.where(hit & (count == slot), square, 0.0)
            count = count + hit.astype(jnp.int32)
        lane = lax.broadcasted_iota(jnp.int32, (1, CAP), 1)
        out = jnp.zeros((1, CAP), jnp.float32)
        for slot in range(CAP):
            out = jnp.where(lane == slot, slots[slot], out)
        slot_ref[...] = (jnp.sqrt(jnp.maximum(out, 0.0)) / math.sqrt(shards * rows * columns)).reshape(1, 1, CAP)


def body(gradient, momentum, owner):
    shards = lax.axis_size("shard")
    devices = shards * lax.axis_size("grp")
    matrices, rows, columns = gradient.shape[1:]
    assert matrices == shards
    element_count = matrices * rows * columns * devices
    width = -(-3 * matrices // LANES) * LANES
    me = lax.axis_index("shard").astype(jnp.int32)
    group = lax.axis_index("grp").astype(jnp.int32)
    grad, mom = gradient[0], momentum[0]
    block = jax.ShapeDtypeStruct((2 * rows, columns), jnp.bfloat16)
    table = jax.ShapeDtypeStruct((devices, width), jnp.float32)
    sums, *payloads = pl.pallas_call(
        functools.partial(pack_kernel, shards),
        name="pack",
        out_shape=[table] + [block] * shards,
        in_specs=[SMEM, ANY, ANY],
        out_specs=[VMEM] * (1 + shards),
        scratch_shapes=[
            pltpu.VMEM((shards, rows, columns), jnp.bfloat16),
            pltpu.VMEM((shards, rows, columns), jnp.float32),
            pltpu.SemaphoreType.DMA((shards,)),
            pltpu.SemaphoreType.DMA((shards,)),
        ],
        compiler_params=pltpu.CompilerParams(vmem_limit_bytes=52 * 2**20),
        cost_estimate=pl.CostEstimate(flops=10 * grad.size, bytes_accessed=10 * grad.size, transcendentals=0),
    )(me[None], grad, mom)
    blocks = [payloads[0]] + [exchange(payloads[step], step, shards) for step in range(1, shards)]
    sums = lax.all_to_all(sums, ("grp", "shard"), 0, 0, tiled=True)
    *ortho, clip = pl.pallas_call(
        functools.partial(newton_kernel, shards, element_count),
        name="newton",
        out_shape=[jax.ShapeDtypeStruct((rows, columns), jnp.bfloat16)] * shards
        + [jax.ShapeDtypeStruct((1, LANES), jnp.float32)],
        in_specs=[VMEM] * (1 + shards),
        out_specs=[VMEM] * (1 + shards),
        scratch_shapes=[pltpu.VMEM((shards * rows, columns), jnp.bfloat16)],
        compiler_params=pltpu.CompilerParams(vmem_limit_bytes=16 * 2**20),
        cost_estimate=pl.CostEstimate(flops=4_000_000_000, bytes_accessed=8 * grad.size, transcendentals=0),
    )(sums, *blocks)
    returned = [ortho[0]] + [exchange(ortho[step], step, shards, back=True) for step in range(1, shards)]
    momentum_out, slot_rms = pl.pallas_call(
        functools.partial(momentum_kernel, shards),
        name="momentum",
        grid=(matrices,),
        out_shape=[
            jax.ShapeDtypeStruct(mom.shape, jnp.float32),
            jax.ShapeDtypeStruct((1, 1, CAP), jnp.float32),
        ],
        in_specs=[
            SMEM,
            SMEM,
            pl.BlockSpec((1, LANES), lambda i: (0, 0)),
            pl.BlockSpec((devices, width), lambda i: (0, 0)),
            pl.BlockSpec((1, rows, columns), lambda i: (i, 0, 0)),
            pl.BlockSpec((1, rows, columns), lambda i: (i, 0, 0)),
        ],
        out_specs=[
            pl.BlockSpec((1, rows, columns), lambda i: (i, 0, 0)),
            pl.BlockSpec((1, 1, CAP), lambda i: (0, 0, 0)),
        ],
        compiler_params=pltpu.CompilerParams(vmem_limit_bytes=8 * 2**20),
        cost_estimate=pl.CostEstimate(flops=4 * grad.size, bytes_accessed=10 * grad.size, transcendentals=0),
    )(jnp.stack([me, group]), owner[0, :, 0], clip, sums, grad, mom)
    update = pl.pallas_call(
        functools.partial(place_kernel, shards),
        name="place",
        out_shape=jax.ShapeDtypeStruct(grad.shape, jnp.bfloat16),
        in_specs=[SMEM] + [VMEM] * shards,
        out_specs=ANY,
        scratch_shapes=[pltpu.SemaphoreType.DMA((shards,))],
        compiler_params=pltpu.CompilerParams(vmem_limit_bytes=8 * 2**20),
        cost_estimate=pl.CostEstimate(flops=0, bytes_accessed=4 * grad.size, transcendentals=0),
    )(me[None], *returned)
    return (update[None], momentum_out[None], slot_rms)


def solution(mesh):
    return jax.shard_map(
        body,
        mesh=mesh,
        in_specs=(
            P("grp", None, "shard", None),
            P("grp", None, "shard", None),
            P("grp", None, None),
        ),
        out_specs=(
            P("grp", None, "shard", None),
            P("grp", None, "shard", None),
            P("grp", "shard", None),
        ),
        check_vma=False,
    )
```

```python
import functools
import math

import jax
import jax.numpy as jnp
from jax import lax
from jax.experimental import pallas as pl
from jax.experimental.pallas import tpu as pltpu
from jax.sharding import PartitionSpec as P

ITERS = 3
CAP = 2
LANES = 128
CHUNK = 24

QUINTIC_A = 3.4445
QUINTIC_B = -4.775
QUINTIC_C = 2.0315
MOMENTUM_DECAY = 0.95
CLIP_LEVEL = 0.5


VMEM = pl.BlockSpec(memory_space=pltpu.VMEM)
SMEM = pl.BlockSpec(memory_space=pltpu.SMEM)
ANY = pl.BlockSpec(memory_space=pl.ANY)


def partner(me, step, shards):
    if shards & (shards - 1) == 0:
        return me ^ step
    return (me + step) % shards


def exchange(block, step, shards, back=False):
    pairs = [(i, partner(i, step, shards)) for i in range(shards)]
    return lax.ppermute(block, "shard", [(b, a) if back else (a, b) for a, b in pairs])


def pack_kernel(shards, grad_hbm, mom_hbm, sums_ref, *rest):
    payloads, (grad_buf, mom_buf, grad_sem, mom_sem) = rest[:shards], rest[shards:]
    rows = grad_hbm.shape[1]
    copies = []
    for step in range(shards):
        target = partner(lax.axis_index("shard"), step, shards)
        for hbm, buf, sem in ((grad_hbm, grad_buf, grad_sem), (mom_hbm, mom_buf, mom_sem)):
            copy = pltpu.make_async_copy(hbm.at[target], buf.at[step], sem.at[step])
            copy.start()
            copies.append(copy)
    lane = lax.broadcasted_iota(jnp.int32, (1, sums_ref.shape[1]), 1)
    sums = jnp.zeros((1, sums_ref.shape[1]), jnp.float32)
    order = list(range(1, shards)) + [0]
    for step in order:
        copies[2 * step].wait()
        copies[2 * step + 1].wait()
        totals = None
        for at in range(0, rows, CHUNK):
            part = pl.ds(at, CHUNK)
            grad_narrow = grad_buf[step, part]
            mom = mom_buf[step, part]
            payloads[step][part] = grad_narrow
            payloads[step][pl.ds(rows + at, CHUNK)] = mom.astype(jnp.bfloat16)
            grad = grad_narrow.astype(jnp.float32)
            terms = [
                jnp.sum(p.reshape(CHUNK // 8, 8, p.shape[1]), axis=0)
                for p in (grad * grad, grad * mom, mom * mom)
            ]
            totals = terms if totals is None else [t + p for t, p in zip(totals, terms)]
        matrix = partner(lax.axis_index("shard"), step, shards)
        for kind, value in enumerate(totals):
            total = jnp.sum(jnp.sum(value, axis=0, keepdims=True), axis=1, keepdims=True)
            sums = jnp.where(lane == matrix + kind * shards, total, sums)
    sums_ref[...] = jnp.broadcast_to(sums, sums_ref.shape)


def lanes_sum(value, keep):
    return jnp.sum(jnp.where(keep, value, 0.0), axis=1, keepdims=True)


def coefficients(sums_ref, shards, element_count):
    sums = sums_ref[...]
    row = lax.broadcasted_iota(jnp.int32, sums.shape, 0)
    lane = lax.broadcasted_iota(jnp.int32, (1, sums.shape[1]), 1)
    first = lax.axis_index("grp") * shards
    every = jnp.sum(sums, axis=0, keepdims=True)
    group = jnp.sum(jnp.where((row >= first) & (row < first + shards), sums, 0.0), axis=0, keepdims=True)
    mean_square = lanes_sum(every, lane < shards) / element_count
    clip = jnp.minimum(jnp.float32(1.0), CLIP_LEVEL / jnp.sqrt(mean_square + 1e-06))
    gg, gm, mm = (lanes_sum(group, lane == lax.axis_index("shard") + kind * shards) for kind in range(3))
    alpha = clip * (1.0 + MOMENTUM_DECAY)
    beta = MOMENTUM_DECAY * MOMENTUM_DECAY
    square_sum = alpha * alpha * gg + (2.0 * beta) * alpha * gm + (beta * beta) * mm
    scale = 1.0 / (jnp.sqrt(jnp.maximum(square_sum, 0.0)) + 1e-07)
    return clip, alpha * scale, beta * scale


def newton_kernel(shards, element_count, sums_ref, *rest):
    blocks, outs, (clip_ref, iterate) = rest[:shards], rest[shards : 2 * shards], rest[2 * shards :]
    rows, columns = outs[0].shape
    clip, alpha, beta = coefficients(sums_ref, shards, element_count)
    clip_ref[...] = jnp.broadcast_to(clip, clip_ref.shape)
    alpha, beta = alpha[0, 0], beta[0, 0]

    for step in range(shards):
        grad = blocks[step][:rows].astype(jnp.float32)
        mom = blocks[step][rows:].astype(jnp.float32)
        iterate[pl.ds(step * rows, rows)] = (alpha * grad + beta * mom).astype(jnp.bfloat16)
    for repeat in range(ITERS):
        last = repeat == ITERS - 1
        gain = math.sqrt(columns) if last else 1.0
        x = iterate[...]
        gram = lax.dot_general(
            x, x, (((1,), (1,)), ((), ())), preferred_element_type=jnp.float32
        ).astype(jnp.bfloat16)
        squared = jnp.dot(gram, gram, preferred_element_type=jnp.float32)
        blended = ((gain * QUINTIC_B) * gram.astype(jnp.float32) + (gain * QUINTIC_C) * squared).astype(jnp.bfloat16)
        product = jnp.dot(blended, x, preferred_element_type=jnp.float32)
        x = ((gain * QUINTIC_A) * x.astype(jnp.float32) + product).astype(jnp.bfloat16)
        if last:
            for step in range(shards):
                outs[step][...] = x[step * rows : (step + 1) * rows]
        else:
            iterate[...] = x


def place_kernel(shards, *rest):
    blocks, (out_hbm, sem) = rest[:shards], rest[shards:]
    copies = []
    for step in range(shards):
        target = partner(lax.axis_index("shard"), step, shards)
        copy = pltpu.make_async_copy(blocks[step], out_hbm.at[target], sem.at[step])
        copy.start()
        copies.append(copy)
    for copy in copies:
        copy.wait()


def momentum_kernel(shards, owner_ref, clip_ref, sums_ref, grad_ref, mom_ref, out_ref, slot_ref):
    rows, columns = grad_ref.shape[1:]
    clip = clip_ref[0, 0]
    out_ref[...] = MOMENTUM_DECAY * mom_ref[...] + clip * grad_ref[...].astype(jnp.float32)

    @pl.when(pl.program_id(0) == 0)
    def _():
        me, group = lax.axis_index("shard"), lax.axis_index("grp")
        row = lax.broadcasted_iota(jnp.int32, sums_ref.shape, 0)
        inside = (row >= group * shards) & (row < (group + 1) * shards)
        sums = jnp.sum(jnp.where(inside, sums_ref[...], 0.0), axis=0, keepdims=True)
        lane = lax.broadcasted_iota(jnp.int32, sums.shape, 1)
        grad_part = clip * (1.0 + MOMENTUM_DECAY)
        mom_part = MOMENTUM_DECAY * MOMENTUM_DECAY
        slots = [jnp.float32(0.0)] * CAP
        count = jnp.int32(0)
        for matrix in range(shards):
            gg, gm, mm = (
                jnp.sum(jnp.where(lane == matrix + kind * shards, sums, 0.0)) for kind in range(3)
            )
            square = grad_part * grad_part * gg + 2.0 * grad_part * mom_part * gm + mom_part * mom_part * mm
            hit = owner_ref[matrix] == me
            for slot in range(CAP):
                slots[slot] = slots[slot] + jnp.where(hit & (count == slot), square, 0.0)
            count = count + hit.astype(jnp.int32)
        lane = lax.broadcasted_iota(jnp.int32, (1, CAP), 1)
        out = jnp.zeros((1, CAP), jnp.float32)
        for slot in range(CAP):
            out = jnp.where(lane == slot, slots[slot], out)
        slot_ref[...] = (jnp.sqrt(jnp.maximum(out, 0.0)) / math.sqrt(shards * rows * columns)).reshape(1, 1, CAP)


def body(gradient, momentum, owner):
    shards = lax.axis_size("shard")
    devices = shards * lax.axis_size("grp")
    matrices, rows, columns = gradient.shape[1:]
    assert matrices == shards
    element_count = matrices * rows * columns * devices
    width = -(-3 * matrices // LANES) * LANES
    grad, mom = gradient[0], momentum[0]
    block = jax.ShapeDtypeStruct((2 * rows, columns), jnp.bfloat16)
    table = jax.ShapeDtypeStruct((devices, width), jnp.float32)
    sums, *payloads = pl.pallas_call(
        functools.partial(pack_kernel, shards),
        name="pack",
        out_shape=[table] + [block] * shards,
        in_specs=[ANY, ANY],
        out_specs=[VMEM] * (1 + shards),
        scratch_shapes=[
            pltpu.VMEM((shards, rows, columns), jnp.bfloat16),
            pltpu.VMEM((shards, rows, columns), jnp.float32),
            pltpu.SemaphoreType.DMA((shards,)),
            pltpu.SemaphoreType.DMA((shards,)),
        ],
        compiler_params=pltpu.CompilerParams(vmem_limit_bytes=52 * 2**20),
        cost_estimate=pl.CostEstimate(flops=10 * grad.size, bytes_accessed=10 * grad.size, transcendentals=0),
    )(grad, mom)
    blocks = [payloads[0]] + [exchange(payloads[step], step, shards) for step in range(1, shards)]
    sums = lax.all_to_all(sums, ("grp", "shard"), 0, 0, tiled=True)
    *ortho, clip = pl.pallas_call(
        functools.partial(newton_kernel, shards, element_count),
        name="newton",
        out_shape=[jax.ShapeDtypeStruct((rows, columns), jnp.bfloat16)] * shards
        + [jax.ShapeDtypeStruct((1, LANES), jnp.float32)],
        in_specs=[VMEM] * (1 + shards),
        out_specs=[VMEM] * (1 + shards),
        scratch_shapes=[pltpu.VMEM((shards * rows, columns), jnp.bfloat16)],
        compiler_params=pltpu.CompilerParams(vmem_limit_bytes=16 * 2**20),
        cost_estimate=pl.CostEstimate(flops=4_000_000_000, bytes_accessed=8 * grad.size, transcendentals=0),
    )(sums, *blocks)
    returned = [ortho[0]] + [exchange(ortho[step], step, shards, back=True) for step in range(1, shards)]
    momentum_out, slot_rms = pl.pallas_call(
        functools.partial(momentum_kernel, shards),
        name="momentum",
        grid=(matrices,),
        out_shape=[
            jax.ShapeDtypeStruct(mom.shape, jnp.float32),
            jax.ShapeDtypeStruct((1, 1, CAP), jnp.float32),
        ],
        in_specs=[
            SMEM,
            pl.BlockSpec((1, LANES), lambda i: (0, 0)),
            pl.BlockSpec((devices, width), lambda i: (0, 0)),
            pl.BlockSpec((1, rows, columns), lambda i: (i, 0, 0)),
            pl.BlockSpec((1, rows, columns), lambda i: (i, 0, 0)),
        ],
        out_specs=[
            pl.BlockSpec((1, rows, columns), lambda i: (i, 0, 0)),
            pl.BlockSpec((1, 1, CAP), lambda i: (0, 0, 0)),
        ],
        compiler_params=pltpu.CompilerParams(vmem_limit_bytes=8 * 2**20),
        cost_estimate=pl.CostEstimate(flops=4 * grad.size, bytes_accessed=10 * grad.size, transcendentals=0),
    )(owner[0, :, 0], clip, sums, grad, mom)
    update = pl.pallas_call(
        functools.partial(place_kernel, shards),
        name="place",
        out_shape=jax.ShapeDtypeStruct(grad.shape, jnp.bfloat16),
        in_specs=[VMEM] * shards,
        out_specs=ANY,
        scratch_shapes=[pltpu.SemaphoreType.DMA((shards,))],
        compiler_params=pltpu.CompilerParams(vmem_limit_bytes=8 * 2**20),
        cost_estimate=pl.CostEstimate(flops=0, bytes_accessed=4 * grad.size, transcendentals=0),
    )(*returned)
    return (update[None], momentum_out[None], slot_rms)


def solution(mesh):
    return jax.shard_map(
        body,
        mesh=mesh,
        in_specs=(
            P("grp", None, "shard", None),
            P("grp", None, "shard", None),
            P("grp", None, None),
        ),
        out_specs=(
            P("grp", None, "shard", None),
            P("grp", None, "shard", None),
            P("grp", "shard", None),
        ),
        check_vma=False,
    )
```

```python
import functools
import math

import jax
import jax.numpy as jnp
from jax import lax
from jax.experimental import pallas as pl
from jax.experimental.pallas import tpu as pltpu
from jax.sharding import PartitionSpec as P

ITERS = 3
CAP = 2
LANES = 128
CHUNK = 24

QUINTIC_A = 3.4445
QUINTIC_B = -4.775
QUINTIC_C = 2.0315
MOMENTUM_DECAY = 0.95
CLIP_LEVEL = 0.5


VMEM = pl.BlockSpec(memory_space=pltpu.VMEM)
SMEM = pl.BlockSpec(memory_space=pltpu.SMEM)
ANY = pl.BlockSpec(memory_space=pl.ANY)


def partner(me, step, shards):
    if shards & (shards - 1) == 0:
        return me ^ step
    return (me + step) % shards


def my_partner(step, shards):
    return partner(lax.axis_index("shard"), step, shards)


def exchange(block, step, shards, back=False):
    pairs = [(i, partner(i, step, shards)) for i in range(shards)]
    return lax.ppermute(block, "shard", [(b, a) if back else (a, b) for a, b in pairs])


def pack_kernel(shards, grad_hbm, mom_hbm, *rest):
    payloads, (mom_buf, grad_sem, mom_sem) = rest[: shards - 1], rest[shards - 1 :]
    rows = grad_hbm.shape[1]
    copies = []
    for step in range(1, shards):
        target = my_partner(step, shards)
        into = payloads[step - 1].at[pl.ds(0, rows)]
        grad_copy = pltpu.make_async_copy(grad_hbm.at[target], into, grad_sem.at[step])
        mom_copy = pltpu.make_async_copy(mom_hbm.at[target], mom_buf.at[step - 1], mom_sem.at[step])
        mom_copy.start()
        grad_copy.start()
        copies.append((grad_copy, mom_copy))
    for step in range(1, shards):
        copies[step - 1][1].wait()
        payloads[step - 1][pl.ds(rows, rows)] = mom_buf[step - 1].astype(jnp.bfloat16)
    for grad_copy, _ in copies:
        grad_copy.wait()


def sums_kernel(shards, grad_hbm, mom_hbm, *rest):
    payloads, (own_ref, sums_ref, mom_buf, sem) = rest[: shards - 1], rest[shards - 1 :]
    rows = grad_hbm.shape[1]
    me = lax.axis_index("shard")
    grad_copy = pltpu.make_async_copy(grad_hbm.at[me], own_ref.at[pl.ds(0, rows)], sem.at[0])
    mom_copy = pltpu.make_async_copy(mom_hbm.at[me], mom_buf, sem.at[1])
    grad_copy.start()
    mom_copy.start()
    lane = lax.broadcasted_iota(jnp.int32, (1, sums_ref.shape[1]), 1)
    sums = jnp.zeros((1, sums_ref.shape[1]), jnp.float32)
    for step in [*range(1, shards), 0]:
        if step == 0:
            grad_copy.wait()
            mom_copy.wait()
            own_ref[pl.ds(rows, rows)] = mom_buf[...].astype(jnp.bfloat16)
        payload = payloads[step - 1] if step else own_ref
        totals = None
        for at in range(0, rows, CHUNK):
            grad = payload[pl.ds(at, CHUNK)].astype(jnp.float32)
            mom = payload[pl.ds(rows + at, CHUNK)].astype(jnp.float32)
            terms = [
                jnp.sum(p.reshape(CHUNK // 8, 8, p.shape[1]), axis=0)
                for p in (grad * grad, grad * mom, mom * mom)
            ]
            totals = terms if totals is None else [t + p for t, p in zip(totals, terms)]
        matrix = my_partner(step, shards)
        for kind, value in enumerate(totals):
            total = jnp.sum(jnp.sum(value, axis=0, keepdims=True), axis=1, keepdims=True)
            sums = jnp.where(lane == matrix + kind * shards, total, sums)
    sums_ref[...] = jnp.broadcast_to(sums, sums_ref.shape)


def lanes_sum(value, keep):
    return jnp.sum(jnp.where(keep, value, 0.0), axis=1, keepdims=True)


def coefficients(sums_ref, shards, element_count):
    sums = sums_ref[...]
    row = lax.broadcasted_iota(jnp.int32, sums.shape, 0)
    lane = lax.broadcasted_iota(jnp.int32, (1, sums.shape[1]), 1)
    first = lax.axis_index("grp") * shards
    every = jnp.sum(sums, axis=0, keepdims=True)
    group = jnp.sum(jnp.where((row >= first) & (row < first + shards), sums, 0.0), axis=0, keepdims=True)
    mean_square = lanes_sum(every, lane < shards) / element_count
    clip = jnp.minimum(jnp.float32(1.0), CLIP_LEVEL / jnp.sqrt(mean_square + 1e-06))
    gg, gm, mm = (lanes_sum(group, lane == lax.axis_index("shard") + kind * shards) for kind in range(3))
    alpha = clip * (1.0 + MOMENTUM_DECAY)
    beta = MOMENTUM_DECAY * MOMENTUM_DECAY
    square_sum = alpha * alpha * gg + (2.0 * beta) * alpha * gm + (beta * beta) * mm
    scale = 1.0 / (jnp.sqrt(jnp.maximum(square_sum, 0.0)) + 1e-07)
    return clip, alpha * scale, beta * scale


def newton_kernel(shards, element_count, sums_ref, *rest):
    blocks, outs, (clip_ref, iterate) = rest[:shards], rest[shards : 2 * shards], rest[2 * shards :]
    rows, columns = outs[0].shape
    clip, alpha, beta = coefficients(sums_ref, shards, element_count)
    clip_ref[...] = jnp.broadcast_to(clip, clip_ref.shape)
    alpha, beta = alpha[0, 0], beta[0, 0]

    for step in range(shards):
        grad = blocks[step][:rows].astype(jnp.float32)
        mom = blocks[step][rows:].astype(jnp.float32)
        iterate[pl.ds(step * rows, rows)] = (alpha * grad + beta * mom).astype(jnp.bfloat16)
    for repeat in range(ITERS):
        last = repeat == ITERS - 1
        gain = math.sqrt(columns) if last else 1.0
        x = iterate[...]
        gram = lax.dot_general(
            x, x, (((1,), (1,)), ((), ())), preferred_element_type=jnp.float32
        ).astype(jnp.bfloat16)
        squared = jnp.dot(gram, gram, preferred_element_type=jnp.float32)
        blended = ((gain * QUINTIC_B) * gram.astype(jnp.float32) + (gain * QUINTIC_C) * squared).astype(jnp.bfloat16)
        product = jnp.dot(blended, x, preferred_element_type=jnp.float32)
        x = ((gain * QUINTIC_A) * x.astype(jnp.float32) + product).astype(jnp.bfloat16)
        if last:
            for step in range(shards):
                outs[step][...] = x[step * rows : (step + 1) * rows]
        else:
            iterate[...] = x


def place_kernel(shards, *rest):
    blocks, (out_hbm, sem) = rest[:shards], rest[shards:]
    copies = []
    for step in range(shards):
        target = my_partner(step, shards)
        copy = pltpu.make_async_copy(blocks[step], out_hbm.at[target], sem.at[step])
        copy.start()
        copies.append(copy)
    for copy in copies:
        copy.wait()


def momentum_kernel(shards, owner_ref, clip_ref, sums_ref, grad_ref, mom_ref, out_ref, slot_ref):
    rows, columns = grad_ref.shape[1:]
    clip = clip_ref[0, 0]
    out_ref[...] = MOMENTUM_DECAY * mom_ref[...] + clip * grad_ref[...].astype(jnp.float32)

    @pl.when(pl.program_id(0) == 0)
    def _():
        me, group = lax.axis_index("shard"), lax.axis_index("grp")
        row = lax.broadcasted_iota(jnp.int32, sums_ref.shape, 0)
        inside = (row >= group * shards) & (row < (group + 1) * shards)
        sums = jnp.sum(jnp.where(inside, sums_ref[...], 0.0), axis=0, keepdims=True)
        lane = lax.broadcasted_iota(jnp.int32, sums.shape, 1)
        grad_part = clip * (1.0 + MOMENTUM_DECAY)
        mom_part = MOMENTUM_DECAY * MOMENTUM_DECAY
        slots = [jnp.float32(0.0)] * CAP
        count = jnp.int32(0)
        for matrix in range(shards):
            gg, gm, mm = (
                jnp.sum(jnp.where(lane == matrix + kind * shards, sums, 0.0)) for kind in range(3)
            )
            square = grad_part * grad_part * gg + 2.0 * grad_part * mom_part * gm + mom_part * mom_part * mm
            hit = owner_ref[matrix] == me
            for slot in range(CAP):
                slots[slot] = slots[slot] + jnp.where(hit & (count == slot), square, 0.0)
            count = count + hit.astype(jnp.int32)
        lane = lax.broadcasted_iota(jnp.int32, (1, CAP), 1)
        out = jnp.zeros((1, CAP), jnp.float32)
        for slot in range(CAP):
            out = jnp.where(lane == slot, slots[slot], out)
        slot_ref[...] = (jnp.sqrt(jnp.maximum(out, 0.0)) / math.sqrt(shards * rows * columns)).reshape(1, 1, CAP)


def body(gradient, momentum, owner):
    shards = lax.axis_size("shard")
    devices = shards * lax.axis_size("grp")
    matrices, rows, columns = gradient.shape[1:]
    assert matrices == shards
    element_count = matrices * rows * columns * devices
    width = -(-3 * matrices // LANES) * LANES
    grad, mom = gradient[0], momentum[0]
    block = jax.ShapeDtypeStruct((2 * rows, columns), jnp.bfloat16)
    table = jax.ShapeDtypeStruct((devices, width), jnp.float32)
    payloads = pl.pallas_call(
        functools.partial(pack_kernel, shards),
        name="pack",
        out_shape=[block] * (shards - 1),
        in_specs=[ANY, ANY],
        out_specs=[VMEM] * (shards - 1),
        scratch_shapes=[
            pltpu.VMEM((shards - 1, rows, columns), jnp.float32),
            pltpu.SemaphoreType.DMA((shards,)),
            pltpu.SemaphoreType.DMA((shards,)),
        ],
        compiler_params=pltpu.CompilerParams(vmem_limit_bytes=105 * 2**19),
        cost_estimate=pl.CostEstimate(flops=grad.size, bytes_accessed=10 * grad.size, transcendentals=0),
    )(grad, mom)
    blocks = [exchange(payload, step, shards) for step, payload in enumerate(payloads, 1)]
    own, sums = pl.pallas_call(
        functools.partial(sums_kernel, shards),
        name="sums",
        out_shape=[block, table],
        in_specs=[ANY, ANY] + [VMEM] * (shards - 1),
        out_specs=[VMEM, VMEM],
        scratch_shapes=[pltpu.VMEM((rows, columns), jnp.float32), pltpu.SemaphoreType.DMA((2,))],
        compiler_params=pltpu.CompilerParams(vmem_limit_bytes=8 * 2**20),
        cost_estimate=pl.CostEstimate(flops=6 * grad.size, bytes_accessed=4 * grad.size, transcendentals=0),
    )(grad, mom, *payloads)
    blocks = [own, *blocks]
    sums = lax.all_to_all(sums, ("grp", "shard"), 0, 0, tiled=True)
    *ortho, clip = pl.pallas_call(
        functools.partial(newton_kernel, shards, element_count),
        name="newton",
        out_shape=[jax.ShapeDtypeStruct((rows, columns), jnp.bfloat16)] * shards
        + [jax.ShapeDtypeStruct((1, LANES), jnp.float32)],
        in_specs=[VMEM] * (1 + shards),
        out_specs=[VMEM] * (1 + shards),
        scratch_shapes=[pltpu.VMEM((shards * rows, columns), jnp.bfloat16)],
        compiler_params=pltpu.CompilerParams(vmem_limit_bytes=16 * 2**20),
        cost_estimate=pl.CostEstimate(flops=4_000_000_000, bytes_accessed=8 * grad.size, transcendentals=0),
    )(sums, *blocks)
    returned = [ortho[0]] + [exchange(ortho[step], step, shards, back=True) for step in range(1, shards)]
    momentum_out, slot_rms = pl.pallas_call(
        functools.partial(momentum_kernel, shards),
        name="momentum",
        grid=(matrices,),
        out_shape=[
            jax.ShapeDtypeStruct(mom.shape, jnp.float32),
            jax.ShapeDtypeStruct((1, 1, CAP), jnp.float32),
        ],
        in_specs=[
            SMEM,
            pl.BlockSpec((1, LANES), lambda i: (0, 0)),
            pl.BlockSpec((devices, width), lambda i: (0, 0)),
            pl.BlockSpec((1, rows, columns), lambda i: (i, 0, 0)),
            pl.BlockSpec((1, rows, columns), lambda i: (i, 0, 0)),
        ],
        out_specs=[
            pl.BlockSpec((1, rows, columns), lambda i: (i, 0, 0)),
            pl.BlockSpec((1, 1, CAP), lambda i: (0, 0, 0)),
        ],
        compiler_params=pltpu.CompilerParams(vmem_limit_bytes=8 * 2**20),
        cost_estimate=pl.CostEstimate(flops=4 * grad.size, bytes_accessed=10 * grad.size, transcendentals=0),
    )(owner[0, :, 0], clip, sums, grad, mom)
    update = pl.pallas_call(
        functools.partial(place_kernel, shards),
        name="place",
        out_shape=jax.ShapeDtypeStruct(grad.shape, jnp.bfloat16),
        in_specs=[VMEM] * shards,
        out_specs=ANY,
        scratch_shapes=[pltpu.SemaphoreType.DMA((shards,))],
        compiler_params=pltpu.CompilerParams(vmem_limit_bytes=8 * 2**20),
        cost_estimate=pl.CostEstimate(flops=0, bytes_accessed=4 * grad.size, transcendentals=0),
    )(*returned)
    return (update[None], momentum_out[None], slot_rms)


def solution(mesh):
    return jax.shard_map(
        body,
        mesh=mesh,
        in_specs=(
            P("grp", None, "shard", None),
            P("grp", None, "shard", None),
            P("grp", None, None),
        ),
        out_specs=(
            P("grp", None, "shard", None),
            P("grp", None, "shard", None),
            P("grp", "shard", None),
        ),
        check_vma=False,
    )
```

```python
import functools
import math

import jax
import jax.numpy as jnp
from jax import lax
from jax.experimental import pallas as pl
from jax.experimental.pallas import tpu as pltpu
from jax.sharding import PartitionSpec as P

ITERS = 3
CAP = 2
LANES = 128
CHUNK = 24

QUINTIC_A = 3.4445
QUINTIC_B = -4.775
QUINTIC_C = 2.0315
MOMENTUM_DECAY = 0.95
CLIP_LEVEL = 0.5


VMEM = pl.BlockSpec(memory_space=pltpu.VMEM)
SMEM = pl.BlockSpec(memory_space=pltpu.SMEM)
ANY = pl.BlockSpec(memory_space=pl.ANY)


def mirrored(step, shards):
    bits = (shards - 1).bit_length() // 2
    if shards != 1 << (2 * bits):
        return step
    return step >> bits | (step & ((1 << bits) - 1)) << bits


def partner(group, me, place, shards):
    step = place % (shards - 1) + 1 if place else 0
    if shards & (shards - 1):
        return (me + step) % shards
    if isinstance(group, int):
        return me ^ (mirrored(step, shards) if group % 2 else step)
    return me ^ (step + (group & 1) * (mirrored(step, shards) - step))


def my_partner(place, shards):
    return partner(lax.axis_index("grp"), lax.axis_index("shard"), place, shards)


def exchange(block, step, shards, back=False):
    pairs = [
        (group * shards + i, group * shards + partner(group, i, step, shards))
        for group in range(lax.axis_size("grp"))
        for i in range(shards)
    ]
    return lax.ppermute(block, ("grp", "shard"), [(b, a) if back else (a, b) for a, b in pairs])


def pack_kernel(shards, grad_hbm, mom_hbm, *rest):
    payloads, (mom_buf, grad_sem, mom_sem) = rest[: shards - 1], rest[shards - 1 :]
    rows = grad_hbm.shape[1]
    copies = []
    for step in range(1, shards):
        target = my_partner(step, shards)
        into = payloads[step - 1].at[pl.ds(0, rows)]
        grad_copy = pltpu.make_async_copy(grad_hbm.at[target], into, grad_sem.at[step])
        mom_copy = pltpu.make_async_copy(mom_hbm.at[target], mom_buf.at[step - 1], mom_sem.at[step])
        mom_copy.start()
        grad_copy.start()
        copies.append((grad_copy, mom_copy))
    for step in range(1, shards):
        copies[step - 1][1].wait()
        payloads[step - 1][pl.ds(rows, rows)] = mom_buf[step - 1].astype(jnp.bfloat16)
    for grad_copy, _ in copies:
        grad_copy.wait()


def sums_kernel(shards, grad_hbm, mom_hbm, *rest):
    payloads, (own_ref, sums_ref, mom_buf, sem) = rest[: shards - 1], rest[shards - 1 :]
    rows = grad_hbm.shape[1]
    me = lax.axis_index("shard")
    grad_copy = pltpu.make_async_copy(grad_hbm.at[me], own_ref.at[pl.ds(0, rows)], sem.at[0])
    mom_copy = pltpu.make_async_copy(mom_hbm.at[me], mom_buf, sem.at[1])
    grad_copy.start()
    mom_copy.start()
    lane = lax.broadcasted_iota(jnp.int32, (1, sums_ref.shape[1]), 1)
    sums = jnp.zeros((1, sums_ref.shape[1]), jnp.float32)
    for step in [*range(1, shards), 0]:
        if step == 0:
            grad_copy.wait()
            mom_copy.wait()
            own_ref[pl.ds(rows, rows)] = mom_buf[...].astype(jnp.bfloat16)
        payload = payloads[step - 1] if step else own_ref
        totals = None
        for at in range(0, rows, CHUNK):
            grad = payload[pl.ds(at, CHUNK)].astype(jnp.float32)
            mom = payload[pl.ds(rows + at, CHUNK)].astype(jnp.float32)
            terms = [
                jnp.sum(p.reshape(CHUNK // 8, 8, p.shape[1]), axis=0)
                for p in (grad * grad, grad * mom, mom * mom)
            ]
            totals = terms if totals is None else [t + p for t, p in zip(totals, terms)]
        matrix = my_partner(step, shards)
        for kind, value in enumerate(totals):
            total = jnp.sum(jnp.sum(value, axis=0, keepdims=True), axis=1, keepdims=True)
            sums = jnp.where(lane == matrix + kind * shards, total, sums)
    sums_ref[...] = jnp.broadcast_to(sums, sums_ref.shape)


def lanes_sum(value, keep):
    return jnp.sum(jnp.where(keep, value, 0.0), axis=1, keepdims=True)


def coefficients(sums_ref, shards, element_count):
    sums = sums_ref[...]
    row = lax.broadcasted_iota(jnp.int32, sums.shape, 0)
    lane = lax.broadcasted_iota(jnp.int32, (1, sums.shape[1]), 1)
    first = lax.axis_index("grp") * shards
    every = jnp.sum(sums, axis=0, keepdims=True)
    group = jnp.sum(jnp.where((row >= first) & (row < first + shards), sums, 0.0), axis=0, keepdims=True)
    mean_square = lanes_sum(every, lane < shards) / element_count
    clip = jnp.minimum(jnp.float32(1.0), CLIP_LEVEL / jnp.sqrt(mean_square + 1e-06))
    gg, gm, mm = (lanes_sum(group, lane == lax.axis_index("shard") + kind * shards) for kind in range(3))
    alpha = clip * (1.0 + MOMENTUM_DECAY)
    beta = MOMENTUM_DECAY * MOMENTUM_DECAY
    square_sum = alpha * alpha * gg + (2.0 * beta) * alpha * gm + (beta * beta) * mm
    scale = 1.0 / (jnp.sqrt(jnp.maximum(square_sum, 0.0)) + 1e-07)
    return clip, alpha * scale, beta * scale


def newton_kernel(shards, element_count, sums_ref, *rest):
    blocks, outs, (clip_ref, iterate) = rest[:shards], rest[shards : 2 * shards], rest[2 * shards :]
    rows, columns = outs[0].shape
    clip, alpha, beta = coefficients(sums_ref, shards, element_count)
    clip_ref[...] = jnp.broadcast_to(clip, clip_ref.shape)
    alpha, beta = alpha[0, 0], beta[0, 0]

    for step in range(shards):
        grad = blocks[step][:rows].astype(jnp.float32)
        mom = blocks[step][rows:].astype(jnp.float32)
        iterate[pl.ds(step * rows, rows)] = (alpha * grad + beta * mom).astype(jnp.bfloat16)
    for repeat in range(ITERS):
        last = repeat == ITERS - 1
        gain = math.sqrt(columns) if last else 1.0
        x = iterate[...]
        gram = lax.dot_general(
            x, x, (((1,), (1,)), ((), ())), preferred_element_type=jnp.float32
        ).astype(jnp.bfloat16)
        squared = jnp.dot(gram, gram, preferred_element_type=jnp.float32)
        blended = ((gain * QUINTIC_B) * gram.astype(jnp.float32) + (gain * QUINTIC_C) * squared).astype(jnp.bfloat16)
        product = jnp.dot(blended, x, preferred_element_type=jnp.float32)
        x = ((gain * QUINTIC_A) * x.astype(jnp.float32) + product).astype(jnp.bfloat16)
        if last:
            for step in range(shards):
                outs[step][...] = x[step * rows : (step + 1) * rows]
        else:
            iterate[...] = x


def place_kernel(steps, shards, *rest):
    blocks, out_hbm, sem = rest[: len(steps)], rest[-2], rest[-1]
    copies = []
    for step, block in zip(steps, blocks):
        copy = pltpu.make_async_copy(block, out_hbm.at[my_partner(step, shards)], sem.at[step])
        copy.start()
        copies.append(copy)
    for copy in copies:
        copy.wait()


def momentum_kernel(shards, owner_ref, clip_ref, sums_ref, grad_ref, mom_ref, out_ref, slot_ref):
    rows, columns = grad_ref.shape[1:]
    clip = clip_ref[0, 0]
    out_ref[...] = MOMENTUM_DECAY * mom_ref[...] + clip * grad_ref[...].astype(jnp.float32)

    @pl.when(pl.program_id(0) == 0)
    def _():
        me, group = lax.axis_index("shard"), lax.axis_index("grp")
        row = lax.broadcasted_iota(jnp.int32, sums_ref.shape, 0)
        inside = (row >= group * shards) & (row < (group + 1) * shards)
        sums = jnp.sum(jnp.where(inside, sums_ref[...], 0.0), axis=0, keepdims=True)
        lane = lax.broadcasted_iota(jnp.int32, sums.shape, 1)
        grad_part = clip * (1.0 + MOMENTUM_DECAY)
        mom_part = MOMENTUM_DECAY * MOMENTUM_DECAY
        slots = [jnp.float32(0.0)] * CAP
        count = jnp.int32(0)
        for matrix in range(shards):
            gg, gm, mm = (
                jnp.sum(jnp.where(lane == matrix + kind * shards, sums, 0.0)) for kind in range(3)
            )
            square = grad_part * grad_part * gg + 2.0 * grad_part * mom_part * gm + mom_part * mom_part * mm
            hit = owner_ref[matrix] == me
            for slot in range(CAP):
                slots[slot] = slots[slot] + jnp.where(hit & (count == slot), square, 0.0)
            count = count + hit.astype(jnp.int32)
        lane = lax.broadcasted_iota(jnp.int32, (1, CAP), 1)
        out = jnp.zeros((1, CAP), jnp.float32)
        for slot in range(CAP):
            out = jnp.where(lane == slot, slots[slot], out)
        slot_ref[...] = (jnp.sqrt(jnp.maximum(out, 0.0)) / math.sqrt(shards * rows * columns)).reshape(1, 1, CAP)


def body(gradient, momentum, owner):
    shards = lax.axis_size("shard")
    devices = shards * lax.axis_size("grp")
    matrices, rows, columns = gradient.shape[1:]
    assert matrices == shards
    element_count = matrices * rows * columns * devices
    width = -(-3 * matrices // LANES) * LANES
    grad, mom = gradient[0], momentum[0]
    block = jax.ShapeDtypeStruct((2 * rows, columns), jnp.bfloat16)
    table = jax.ShapeDtypeStruct((devices, width), jnp.float32)
    payloads = pl.pallas_call(
        functools.partial(pack_kernel, shards),
        name="pack",
        out_shape=[block] * (shards - 1),
        in_specs=[ANY, ANY],
        out_specs=[VMEM] * (shards - 1),
        scratch_shapes=[
            pltpu.VMEM((shards - 1, rows, columns), jnp.float32),
            pltpu.SemaphoreType.DMA((shards,)),
            pltpu.SemaphoreType.DMA((shards,)),
        ],
        compiler_params=pltpu.CompilerParams(vmem_limit_bytes=105 * 2**19),
        cost_estimate=pl.CostEstimate(flops=grad.size, bytes_accessed=10 * grad.size, transcendentals=0),
    )(grad, mom)
    blocks = [exchange(payload, step, shards) for step, payload in enumerate(payloads, 1)]
    own, sums = pl.pallas_call(
        functools.partial(sums_kernel, shards),
        name="sums",
        out_shape=[block, table],
        in_specs=[ANY, ANY] + [VMEM] * (shards - 1),
        out_specs=[VMEM, VMEM],
        scratch_shapes=[pltpu.VMEM((rows, columns), jnp.float32), pltpu.SemaphoreType.DMA((2,))],
        compiler_params=pltpu.CompilerParams(vmem_limit_bytes=102 * 2**19),
        cost_estimate=pl.CostEstimate(flops=6 * grad.size, bytes_accessed=4 * grad.size, transcendentals=0),
    )(grad, mom, *payloads)
    blocks = [own, *blocks]
    sums = lax.all_to_all(sums, ("grp", "shard"), 0, 0, tiled=True)
    *ortho, clip = pl.pallas_call(
        functools.partial(newton_kernel, shards, element_count),
        name="newton",
        out_shape=[jax.ShapeDtypeStruct((rows, columns), jnp.bfloat16)] * shards
        + [jax.ShapeDtypeStruct((1, LANES), jnp.float32)],
        in_specs=[VMEM] * (1 + shards),
        out_specs=[VMEM] * (1 + shards),
        scratch_shapes=[pltpu.VMEM((shards * rows, columns), jnp.bfloat16)],
        compiler_params=pltpu.CompilerParams(vmem_limit_bytes=16 * 2**20),
        cost_estimate=pl.CostEstimate(flops=4_000_000_000, bytes_accessed=8 * grad.size, transcendentals=0),
    )(sums, *blocks)
    returned = [ortho[0]] + [exchange(ortho[step], step, shards, back=True) for step in range(1, shards)]
    momentum_out, slot_rms = pl.pallas_call(
        functools.partial(momentum_kernel, shards),
        name="momentum",
        grid=(matrices,),
        out_shape=[
            jax.ShapeDtypeStruct(mom.shape, jnp.float32),
            jax.ShapeDtypeStruct((1, 1, CAP), jnp.float32),
        ],
        in_specs=[
            SMEM,
            pl.BlockSpec((1, LANES), lambda i: (0, 0)),
            pl.BlockSpec((devices, width), lambda i: (0, 0)),
            pl.BlockSpec((1, rows, columns), lambda i: (i, 0, 0)),
            pl.BlockSpec((1, rows, columns), lambda i: (i, 0, 0)),
        ],
        out_specs=[
            pl.BlockSpec((1, rows, columns), lambda i: (i, 0, 0)),
            pl.BlockSpec((1, 1, CAP), lambda i: (0, 0, 0)),
        ],
        compiler_params=pltpu.CompilerParams(vmem_limit_bytes=8 * 2**20),
        cost_estimate=pl.CostEstimate(flops=4 * grad.size, bytes_accessed=10 * grad.size, transcendentals=0),
    )(owner[0, :, 0], clip, sums, grad, mom)
    update = None
    for steps in (range(shards - 1), range(shards - 1, shards)):
        earlier = [] if update is None else [update]
        update = pl.pallas_call(
            functools.partial(place_kernel, steps, shards),
            name="place",
            out_shape=jax.ShapeDtypeStruct(grad.shape, jnp.bfloat16),
            in_specs=[VMEM] * len(steps) + [ANY] * len(earlier),
            out_specs=ANY,
            input_output_aliases={len(steps): 0} if earlier else {},
            scratch_shapes=[pltpu.SemaphoreType.DMA((shards,))],
            compiler_params=pltpu.CompilerParams(vmem_limit_bytes=8 * 2**20),
            cost_estimate=pl.CostEstimate(flops=0, bytes_accessed=len(steps) * grad.size, transcendentals=0),
        )(*(returned[step] for step in steps), *earlier)
    return (update[None], momentum_out[None], slot_rms)


def solution(mesh):
    return jax.shard_map(
        body,
        mesh=mesh,
        in_specs=(
            P("grp", None, "shard", None),
            P("grp", None, "shard", None),
            P("grp", None, None),
        ),
        out_specs=(
            P("grp", None, "shard", None),
            P("grp", None, "shard", None),
            P("grp", "shard", None),
        ),
        check_vma=False,
    )
```

```python
import functools
import math

import jax
import jax.numpy as jnp
from jax import lax
from jax.experimental import pallas as pl
from jax.experimental.pallas import tpu as pltpu
from jax.sharding import PartitionSpec as P


ITERS = 3
CAP = 2
LANES = 128
CHUNK = 24

QUINTIC_A = 3.4445
QUINTIC_B = -4.775
QUINTIC_C = 2.0315
MOMENTUM_DECAY = 0.95
CLIP_LEVEL = 0.5


VMEM = pl.BlockSpec(memory_space=pltpu.VMEM)
SMEM = pl.BlockSpec(memory_space=pltpu.SMEM)
ANY = pl.BlockSpec(memory_space=pl.ANY)


def mirrored(step, shards):
    bits = (shards - 1).bit_length() // 2
    if shards != 1 << (2 * bits):
        return step
    return step >> bits | (step & ((1 << bits) - 1)) << bits


def partner(group, me, place, shards):
    step = place % (shards - 1) + 1 if place else 0
    if shards & (shards - 1):
        return (me + step) % shards
    if isinstance(group, int):
        return me ^ (mirrored(step, shards) if group % 2 else step)
    return me ^ (step + (group & 1) * (mirrored(step, shards) - step))


def my_partner(place, shards):
    return partner(lax.axis_index("grp"), lax.axis_index("shard"), place, shards)


def exchange(block, step, shards, back=False):
    pairs = [
        (group * shards + i, group * shards + partner(group, i, step, shards))
        for group in range(lax.axis_size("grp"))
        for i in range(shards)
    ]
    return lax.ppermute(block, ("grp", "shard"), [(b, a) if back else (a, b) for a, b in pairs])


def pack_kernel(steps, shards, grad_hbm, mom_hbm, *rest):
    payloads, (mom_buf, grad_sem, mom_sem) = rest[: len(steps)], rest[-3:]
    rows = grad_hbm.shape[1]
    copies = []
    for at, step in enumerate(steps):
        target = my_partner(step, shards)
        into = payloads[at].at[pl.ds(0, rows)]
        grad_copy = pltpu.make_async_copy(grad_hbm.at[target], into, grad_sem.at[at])
        mom_copy = pltpu.make_async_copy(mom_hbm.at[target], mom_buf.at[at], mom_sem.at[at])
        mom_copy.start()
        grad_copy.start()
        copies.append((grad_copy, mom_copy))
    for at in range(len(steps)):
        copies[at][1].wait()
        payloads[at][pl.ds(rows, rows)] = mom_buf[at].astype(jnp.bfloat16)
    for grad_copy, _ in copies:
        grad_copy.wait()


def sums_kernel(shards, grad_hbm, mom_hbm, *rest):
    payloads, (own_ref, sums_ref, mom_buf, sem) = rest[: shards - 1], rest[shards - 1 :]
    rows = grad_hbm.shape[1]
    me = lax.axis_index("shard")
    grad_copy = pltpu.make_async_copy(grad_hbm.at[me], own_ref.at[pl.ds(0, rows)], sem.at[0])
    mom_copy = pltpu.make_async_copy(mom_hbm.at[me], mom_buf, sem.at[1])
    grad_copy.start()
    mom_copy.start()
    lane = lax.broadcasted_iota(jnp.int32, (1, sums_ref.shape[1]), 1)
    sums = jnp.zeros((1, sums_ref.shape[1]), jnp.float32)
    for step in [*range(1, shards), 0]:
        if step == 0:
            grad_copy.wait()
            mom_copy.wait()
            own_ref[pl.ds(rows, rows)] = mom_buf[...].astype(jnp.bfloat16)
        payload = payloads[step - 1] if step else own_ref
        totals = None
        for at in range(0, rows, CHUNK):
            grad = payload[pl.ds(at, CHUNK)].astype(jnp.float32)
            mom = payload[pl.ds(rows + at, CHUNK)].astype(jnp.float32)
            terms = [
                jnp.sum(p.reshape(CHUNK // 8, 8, p.shape[1]), axis=0)
                for p in (grad * grad, grad * mom, mom * mom)
            ]
            totals = terms if totals is None else [t + p for t, p in zip(totals, terms)]
        matrix = my_partner(step, shards)
        for kind, value in enumerate(totals):
            total = jnp.sum(jnp.sum(value, axis=0, keepdims=True), axis=1, keepdims=True)
            sums = jnp.where(lane == matrix + kind * shards, total, sums)
    sums_ref[...] = jnp.broadcast_to(sums, sums_ref.shape)


def lanes_sum(value, keep):
    return jnp.sum(jnp.where(keep, value, 0.0), axis=1, keepdims=True)


def coefficients(sums_ref, shards, element_count):
    sums = sums_ref[...]
    row = lax.broadcasted_iota(jnp.int32, sums.shape, 0)
    lane = lax.broadcasted_iota(jnp.int32, (1, sums.shape[1]), 1)
    first = lax.axis_index("grp") * shards
    every = jnp.sum(sums, axis=0, keepdims=True)
    group = jnp.sum(jnp.where((row >= first) & (row < first + shards), sums, 0.0), axis=0, keepdims=True)
    mean_square = lanes_sum(every, lane < shards) / element_count
    clip = jnp.minimum(jnp.float32(1.0), CLIP_LEVEL / jnp.sqrt(mean_square + 1e-06))
    gg, gm, mm = (lanes_sum(group, lane == lax.axis_index("shard") + kind * shards) for kind in range(3))
    alpha = clip * (1.0 + MOMENTUM_DECAY)
    beta = MOMENTUM_DECAY * MOMENTUM_DECAY
    square_sum = alpha * alpha * gg + (2.0 * beta) * alpha * gm + (beta * beta) * mm
    scale = 1.0 / (jnp.sqrt(jnp.maximum(square_sum, 0.0)) + 1e-07)
    return clip, alpha * scale, beta * scale


def step_of(blended, iterate, first, rows, gain):
    at = pl.ds(first, rows)
    product = jnp.dot(blended[at], iterate[...], preferred_element_type=jnp.float32)
    return ((gain * QUINTIC_A) * iterate[at].astype(jnp.float32) + product).astype(jnp.bfloat16)


def newton_kernel(shards, element_count, sums_ref, *rest):
    blocks, (first_ref, clip_ref, blended, iterate) = rest[:shards], rest[shards:]
    rows, columns = first_ref.shape
    clip, alpha, beta = coefficients(sums_ref, shards, element_count)
    clip_ref[...] = jnp.broadcast_to(clip, clip_ref.shape)
    alpha, beta = alpha[0, 0], beta[0, 0]
    for at in range(shards):
        grad = blocks[at][:rows].astype(jnp.float32)
        mom = blocks[at][rows:].astype(jnp.float32)
        iterate[pl.ds(at * rows, rows)] = (alpha * grad + beta * mom).astype(jnp.bfloat16)
    for repeat in range(ITERS):
        last = repeat == ITERS - 1
        gain = math.sqrt(columns) if last else 1.0
        x = iterate[...]
        gram = lax.dot_general(
            x, x, (((1,), (1,)), ((), ())), preferred_element_type=jnp.float32
        ).astype(jnp.bfloat16)
        squared = jnp.dot(gram, gram, preferred_element_type=jnp.float32)
        blended[...] = (
            (gain * QUINTIC_B) * gram.astype(jnp.float32) + (gain * QUINTIC_C) * squared
        ).astype(jnp.bfloat16)
        if last:
            first_ref[...] = step_of(blended, iterate, 0, rows, gain)
        else:
            iterate[...] = step_of(blended, iterate, 0, shards * rows, gain)


def apply_kernel(shards, blended, iterate, *outs):
    rows, columns = outs[0].shape
    x = step_of(blended, iterate, rows, (shards - 1) * rows, math.sqrt(columns))
    for at, out in enumerate(outs):
        out[...] = x[at * rows : (at + 1) * rows]


def place_kernel(steps, shards, *rest):
    blocks, out_hbm, sem = rest[: len(steps)], rest[-2], rest[-1]
    copies = []
    for step, block in zip(steps, blocks):
        copy = pltpu.make_async_copy(block, out_hbm.at[my_partner(step, shards)], sem.at[step])
        copy.start()
        copies.append(copy)
    for copy in copies:
        copy.wait()


def momentum_kernel(shards, owner_ref, clip_ref, sums_ref, grad_ref, mom_ref, out_ref, slot_ref):
    rows, columns = grad_ref.shape[1:]
    clip = clip_ref[0, 0]
    out_ref[...] = MOMENTUM_DECAY * mom_ref[...] + clip * grad_ref[...].astype(jnp.float32)

    @pl.when(pl.program_id(0) == 0)
    def _():
        me, group = lax.axis_index("shard"), lax.axis_index("grp")
        row = lax.broadcasted_iota(jnp.int32, sums_ref.shape, 0)
        inside = (row >= group * shards) & (row < (group + 1) * shards)
        sums = jnp.sum(jnp.where(inside, sums_ref[...], 0.0), axis=0, keepdims=True)
        lane = lax.broadcasted_iota(jnp.int32, sums.shape, 1)
        grad_part = clip * (1.0 + MOMENTUM_DECAY)
        mom_part = MOMENTUM_DECAY * MOMENTUM_DECAY
        slots = [jnp.float32(0.0)] * CAP
        count = jnp.int32(0)
        for matrix in range(shards):
            gg, gm, mm = (
                jnp.sum(jnp.where(lane == matrix + kind * shards, sums, 0.0)) for kind in range(3)
            )
            square = grad_part * grad_part * gg + 2.0 * grad_part * mom_part * gm + mom_part * mom_part * mm
            hit = owner_ref[matrix] == me
            for slot in range(CAP):
                slots[slot] = slots[slot] + jnp.where(hit & (count == slot), square, 0.0)
            count = count + hit.astype(jnp.int32)
        lane = lax.broadcasted_iota(jnp.int32, (1, CAP), 1)
        out = jnp.zeros((1, CAP), jnp.float32)
        for slot in range(CAP):
            out = jnp.where(lane == slot, slots[slot], out)
        slot_ref[...] = (jnp.sqrt(jnp.maximum(out, 0.0)) / math.sqrt(shards * rows * columns)).reshape(1, 1, CAP)


def body(gradient, momentum, owner):
    shards = lax.axis_size("shard")
    devices = shards * lax.axis_size("grp")
    matrices, rows, columns = gradient.shape[1:]
    assert matrices == shards
    element_count = matrices * rows * columns * devices
    width = -(-3 * matrices // LANES) * LANES
    grad, mom = gradient[0], momentum[0]
    block = jax.ShapeDtypeStruct((2 * rows, columns), jnp.bfloat16)
    table = jax.ShapeDtypeStruct((devices, width), jnp.float32)
    payloads = []
    for steps in (range(1, 2), range(2, shards)):
        payloads += pl.pallas_call(
            functools.partial(pack_kernel, steps, shards),
            name="pack",
            out_shape=[block] * len(steps),
            in_specs=[ANY, ANY],
            out_specs=[VMEM] * len(steps),
            scratch_shapes=[
                pltpu.VMEM((len(steps), rows, columns), jnp.float32),
                pltpu.SemaphoreType.DMA((len(steps),)),
                pltpu.SemaphoreType.DMA((len(steps),)),
            ],
            compiler_params=pltpu.CompilerParams(vmem_limit_bytes=106 * 2**19),
            cost_estimate=pl.CostEstimate(
                flops=len(steps) * rows * columns, bytes_accessed=10 * len(steps) * rows * columns, transcendentals=0
            ),
        )(grad, mom)
    blocks = [exchange(payload, step, shards) for step, payload in enumerate(payloads[:-1], 1)]
    blocks.append(exchange(payloads[-1], shards - 1, shards))
    own, sums = pl.pallas_call(
        functools.partial(sums_kernel, shards),
        name="sums",
        out_shape=[block, table],
        in_specs=[ANY, ANY] + [VMEM] * (shards - 1),
        out_specs=[VMEM, VMEM],
        scratch_shapes=[pltpu.VMEM((rows, columns), jnp.float32), pltpu.SemaphoreType.DMA((2,))],
        compiler_params=pltpu.CompilerParams(vmem_limit_bytes=102 * 2**19),
        cost_estimate=pl.CostEstimate(flops=6 * grad.size, bytes_accessed=4 * grad.size, transcendentals=0),
    )(grad, mom, *payloads)
    blocks = [own, *blocks]
    sums = lax.all_to_all(sums, ("grp", "shard"), 0, 0, tiled=True)
    side = shards * rows
    part = jax.ShapeDtypeStruct((rows, columns), jnp.bfloat16)
    first, clip, blended, iterate = pl.pallas_call(
        functools.partial(newton_kernel, shards, element_count),
        name="newton",
        out_shape=[
            part,
            jax.ShapeDtypeStruct((1, LANES), jnp.float32),
            jax.ShapeDtypeStruct((side, side), jnp.bfloat16),
            jax.ShapeDtypeStruct((side, columns), jnp.bfloat16),
        ],
        in_specs=[VMEM] * (1 + shards),
        out_specs=[VMEM] * 4,
        compiler_params=pltpu.CompilerParams(vmem_limit_bytes=16 * 2**20),
        cost_estimate=pl.CostEstimate(flops=4_000_000_000, bytes_accessed=8 * grad.size, transcendentals=0),
    )(sums, blocks[1], blocks[0], *blocks[2:])
    returned = {1: exchange(first, 1, shards, back=True)}
    own, *others = pl.pallas_call(
        functools.partial(apply_kernel, shards),
        name="apply",
        out_shape=[part] * (shards - 1),
        in_specs=[VMEM] * 2,
        out_specs=[VMEM] * (shards - 1),
        compiler_params=pltpu.CompilerParams(vmem_limit_bytes=16 * 2**20),
        cost_estimate=pl.CostEstimate(flops=400_000_000, bytes_accessed=4 * grad.size, transcendentals=0),
    )(blended, iterate)
    returned = {0: own, **returned, **{step: exchange(x, step, shards, back=True) for step, x in enumerate(others, 2)}}
    momentum_out, slot_rms = pl.pallas_call(
        functools.partial(momentum_kernel, shards),
        name="momentum",
        grid=(matrices,),
        out_shape=[
            jax.ShapeDtypeStruct(mom.shape, jnp.float32),
            jax.ShapeDtypeStruct((1, 1, CAP), jnp.float32),
        ],
        in_specs=[
            SMEM,
            pl.BlockSpec((1, LANES), lambda i: (0, 0)),
            pl.BlockSpec((devices, width), lambda i: (0, 0)),
            pl.BlockSpec((1, rows, columns), lambda i: (i, 0, 0)),
            pl.BlockSpec((1, rows, columns), lambda i: (i, 0, 0)),
        ],
        out_specs=[
            pl.BlockSpec((1, rows, columns), lambda i: (i, 0, 0)),
            pl.BlockSpec((1, 1, CAP), lambda i: (0, 0, 0)),
        ],
        compiler_params=pltpu.CompilerParams(vmem_limit_bytes=8 * 2**20),
        cost_estimate=pl.CostEstimate(flops=4 * grad.size, bytes_accessed=10 * grad.size, transcendentals=0),
    )(owner[0, :, 0], clip, sums, grad, mom)
    update = None
    for steps in (range(shards - 1), range(shards - 1, shards)):
        earlier = [] if update is None else [update]
        update = pl.pallas_call(
            functools.partial(place_kernel, steps, shards),
            name="place",
            out_shape=jax.ShapeDtypeStruct(grad.shape, jnp.bfloat16),
            in_specs=[VMEM] * len(steps) + [ANY] * len(earlier),
            out_specs=ANY,
            input_output_aliases={len(steps): 0} if earlier else {},
            scratch_shapes=[pltpu.SemaphoreType.DMA((shards,))],
            compiler_params=pltpu.CompilerParams(vmem_limit_bytes=8 * 2**20),
            cost_estimate=pl.CostEstimate(flops=0, bytes_accessed=len(steps) * grad.size, transcendentals=0),
        )(*(returned[step] for step in steps), *earlier)
    return (update[None], momentum_out[None], slot_rms)


def solution(mesh):
    return jax.shard_map(
        body,
        mesh=mesh,
        in_specs=(
            P("grp", None, "shard", None),
            P("grp", None, "shard", None),
            P("grp", None, None),
        ),
        out_specs=(
            P("grp", None, "shard", None),
            P("grp", None, "shard", None),
            P("grp", "shard", None),
        ),
        check_vma=False,
    )
```

```python
import functools
import math

import jax
import jax.numpy as jnp
from jax import lax
from jax.experimental import pallas as pl
from jax.experimental.pallas import tpu as pltpu
from jax.sharding import PartitionSpec as P


ITERS = 3
CAP = 2
LANES = 128
CHUNK = 24

QUINTIC_A = 3.4445
QUINTIC_B = -4.775
QUINTIC_C = 2.0315
MOMENTUM_DECAY = 0.95
CLIP_LEVEL = 0.5


VMEM = pl.BlockSpec(memory_space=pltpu.VMEM)
SMEM = pl.BlockSpec(memory_space=pltpu.SMEM)
ANY = pl.BlockSpec(memory_space=pl.ANY)


def mirrored(step, shards):
    bits = (shards - 1).bit_length() // 2
    if shards != 1 << (2 * bits):
        return step
    return step >> bits | (step & ((1 << bits) - 1)) << bits


def partner(group, me, place, shards):
    step = place % (shards - 1) + 1 if place else 0
    if shards & (shards - 1):
        return (me + step) % shards
    if isinstance(group, int):
        return me ^ (mirrored(step, shards) if group % 2 else step)
    return me ^ (step + (group & 1) * (mirrored(step, shards) - step))


def my_partner(place, shards):
    return partner(lax.axis_index("grp"), lax.axis_index("shard"), place, shards)


def exchange(block, step, shards, back=False):
    pairs = [
        (group * shards + i, group * shards + partner(group, i, step, shards))
        for group in range(lax.axis_size("grp"))
        for i in range(shards)
    ]
    return lax.ppermute(block, ("grp", "shard"), [(b, a) if back else (a, b) for a, b in pairs])


def pack_kernel(steps, shards, grad_hbm, mom_hbm, *rest):
    payloads, (mom_buf, grad_sem, mom_sem) = rest[: len(steps)], rest[-3:]
    apart = rest[len(steps) : -3]
    rows = grad_hbm.shape[1]
    copies = []
    for at, step in enumerate(steps):
        target = my_partner(step, shards)
        into = payloads[at].at[pl.ds(0, rows)]
        grad_copy = pltpu.make_async_copy(grad_hbm.at[target], into, grad_sem.at[at])
        mom_copy = pltpu.make_async_copy(mom_hbm.at[target], mom_buf.at[at], mom_sem.at[at])
        mom_copy.start()
        grad_copy.start()
        copies.append((grad_copy, mom_copy))
    for at in range(len(steps)):
        copies[at][1].wait()
        into = apart[0] if steps[at] == shards - 1 else payloads[at].at[pl.ds(rows, rows)]
        into[...] = mom_buf[at].astype(jnp.bfloat16)
    for grad_copy, _ in copies:
        grad_copy.wait()


def sums_kernel(shards, *rest):
    payloads, apart, sums_ref = rest[:shards], rest[shards], rest[shards + 1]
    rows = payloads[0].shape[0] // 2
    lane = lax.broadcasted_iota(jnp.int32, (1, sums_ref.shape[1]), 1)
    sums = jnp.zeros((1, sums_ref.shape[1]), jnp.float32)
    for step, payload in enumerate(payloads):
        totals = None
        for at in range(0, rows, CHUNK):
            grad = payload[pl.ds(at, CHUNK)].astype(jnp.float32)
            mom = (apart[pl.ds(at, CHUNK)] if step == shards - 1 else payload[pl.ds(rows + at, CHUNK)]).astype(jnp.float32)
            terms = [
                jnp.sum(p.reshape(CHUNK // 8, 8, p.shape[1]), axis=0)
                for p in (grad * grad, grad * mom, mom * mom)
            ]
            totals = terms if totals is None else [t + p for t, p in zip(totals, terms)]
        matrix = my_partner(step, shards)
        for kind, value in enumerate(totals):
            total = jnp.sum(jnp.sum(value, axis=0, keepdims=True), axis=1, keepdims=True)
            sums = jnp.where(lane == matrix + kind * shards, total, sums)
    sums_ref[...] = jnp.broadcast_to(sums, sums_ref.shape)


def lanes_sum(value, keep):
    return jnp.sum(jnp.where(keep, value, 0.0), axis=1, keepdims=True)


def coefficients(sums_ref, shards, element_count):
    sums = sums_ref[...]
    row = lax.broadcasted_iota(jnp.int32, sums.shape, 0)
    lane = lax.broadcasted_iota(jnp.int32, (1, sums.shape[1]), 1)
    first = lax.axis_index("grp") * shards
    every = jnp.sum(sums, axis=0, keepdims=True)
    group = jnp.sum(jnp.where((row >= first) & (row < first + shards), sums, 0.0), axis=0, keepdims=True)
    mean_square = lanes_sum(every, lane < shards) / element_count
    clip = jnp.minimum(jnp.float32(1.0), CLIP_LEVEL / jnp.sqrt(mean_square + 1e-06))
    gg, gm, mm = (lanes_sum(group, lane == lax.axis_index("shard") + kind * shards) for kind in range(3))
    alpha = clip * (1.0 + MOMENTUM_DECAY)
    beta = MOMENTUM_DECAY * MOMENTUM_DECAY
    square_sum = alpha * alpha * gg + (2.0 * beta) * alpha * gm + (beta * beta) * mm
    scale = 1.0 / (jnp.sqrt(jnp.maximum(square_sum, 0.0)) + 1e-07)
    return clip, alpha * scale, beta * scale


def iterate_rows(block, alpha, beta, rows):
    return (alpha * block[:rows].astype(jnp.float32) + beta * block[rows:].astype(jnp.float32)).astype(jnp.bfloat16)


def gram_of(left, right):
    return lax.dot_general(left, right, (((1,), (1,)), ((), ())), preferred_element_type=jnp.float32).astype(jnp.bfloat16)


def step_of(blended, iterate, first, rows, gain):
    at = pl.ds(first, rows)
    product = jnp.dot(blended[at], iterate[...], preferred_element_type=jnp.float32)
    return ((gain * QUINTIC_A) * iterate[at].astype(jnp.float32) + product).astype(jnp.bfloat16)


def begin_kernel(shards, element_count, cut, sums_ref, *rest):
    blocks, (factors_ref, x_ref, gram_ref) = rest[: shards - 1], rest[shards - 1 :]
    rows = blocks[0].shape[0] // 2
    factors = coefficients(sums_ref, shards, element_count)
    for at, factor in enumerate(factors):
        factors_ref[pl.ds(at, 1)] = jnp.broadcast_to(factor, (1, LANES))
    _, alpha, beta = (factor[0, 0] for factor in factors)
    for at, block in enumerate(blocks):
        x_ref[pl.ds(at * rows, rows)] = iterate_rows(block, alpha, beta, rows)
    gram_ref[...] = gram_of(x_ref[...], x_ref[cut - rows :])


def newton_kernel(cut, factors_ref, last_grad, last_mom, x_ref, gram_ref, early_ref, blended, iterate):
    rows, columns = early_ref.shape
    size = iterate.shape[0]
    iterate[pl.ds(0, rows)] = (
        factors_ref[1, 0] * last_grad[...].astype(jnp.float32) + factors_ref[2, 0] * last_mom[...].astype(jnp.float32)
    ).astype(jnp.bfloat16)
    iterate[pl.ds(rows, size - rows)] = x_ref[...]
    for repeat in range(ITERS):
        last = repeat == ITERS - 1
        gain = math.sqrt(columns) if last else 1.0
        x = iterate[...]
        if repeat == 0:
            below = jnp.concatenate([gram_of(x[rows:], x[:cut]), gram_ref[...]], axis=1)
            gram = jnp.concatenate([gram_of(x[:rows], x), below], axis=0)
        else:
            gram = gram_of(x, x)
        squared = jnp.dot(gram, gram, preferred_element_type=jnp.float32)
        blended[...] = (
            (gain * QUINTIC_B) * gram.astype(jnp.float32) + (gain * QUINTIC_C) * squared
        ).astype(jnp.bfloat16)
        if last:
            early_ref[...] = step_of(blended, iterate, rows, rows, gain)
        else:
            iterate[...] = step_of(blended, iterate, 0, size, gain)


def apply_kernel(blended, iterate, *outs):
    rows, columns = outs[0].shape
    gain = math.sqrt(columns)
    outs[0][...] = step_of(blended, iterate, 0, rows, gain)
    x = step_of(blended, iterate, 2 * rows, (len(outs) - 1) * rows, gain)
    for at, out in enumerate(outs[1:]):
        out[...] = x[at * rows : (at + 1) * rows]


def place_kernel(steps, shards, *rest):
    blocks, out_hbm, sem = rest[: len(steps)], rest[-2], rest[-1]
    copies = []
    for step, block in zip(steps, blocks):
        copy = pltpu.make_async_copy(block, out_hbm.at[my_partner(step, shards)], sem.at[step])
        copy.start()
        copies.append(copy)
    for copy in copies:
        copy.wait()


def momentum_kernel(shards, owner_ref, factors_ref, sums_ref, grad_ref, mom_ref, out_ref, slot_ref):
    rows, columns = grad_ref.shape[1:]
    clip = factors_ref[0, 0]
    out_ref[...] = MOMENTUM_DECAY * mom_ref[...] + clip * grad_ref[...].astype(jnp.float32)

    @pl.when(pl.program_id(0) == 0)
    def _():
        me, group = lax.axis_index("shard"), lax.axis_index("grp")
        row = lax.broadcasted_iota(jnp.int32, sums_ref.shape, 0)
        inside = (row >= group * shards) & (row < (group + 1) * shards)
        sums = jnp.sum(jnp.where(inside, sums_ref[...], 0.0), axis=0, keepdims=True)
        lane = lax.broadcasted_iota(jnp.int32, sums.shape, 1)
        grad_part = clip * (1.0 + MOMENTUM_DECAY)
        mom_part = MOMENTUM_DECAY * MOMENTUM_DECAY
        slots = [jnp.float32(0.0)] * CAP
        count = jnp.int32(0)
        for matrix in range(shards):
            gg, gm, mm = (
                jnp.sum(jnp.where(lane == matrix + kind * shards, sums, 0.0)) for kind in range(3)
            )
            square = grad_part * grad_part * gg + 2.0 * grad_part * mom_part * gm + mom_part * mom_part * mm
            hit = owner_ref[matrix] == me
            for slot in range(CAP):
                slots[slot] = slots[slot] + jnp.where(hit & (count == slot), square, 0.0)
            count = count + hit.astype(jnp.int32)
        lane = lax.broadcasted_iota(jnp.int32, (1, CAP), 1)
        out = jnp.zeros((1, CAP), jnp.float32)
        for slot in range(CAP):
            out = jnp.where(lane == slot, slots[slot], out)
        slot_ref[...] = (jnp.sqrt(jnp.maximum(out, 0.0)) / math.sqrt(shards * rows * columns)).reshape(1, 1, CAP)


def body(gradient, momentum, owner):
    shards = lax.axis_size("shard")
    devices = shards * lax.axis_size("grp")
    matrices, rows, columns = gradient.shape[1:]
    assert matrices == shards
    element_count = matrices * rows * columns * devices
    width = -(-3 * matrices // LANES) * LANES
    grad, mom = gradient[0], momentum[0]
    block = jax.ShapeDtypeStruct((2 * rows, columns), jnp.bfloat16)
    half = jax.ShapeDtypeStruct((rows, columns), jnp.bfloat16)
    table = jax.ShapeDtypeStruct((devices, width), jnp.float32)
    payloads = []
    for steps, limit in (([1], 106), ([*range(2, shards), 0], 105)):
        payloads += pl.pallas_call(
            functools.partial(pack_kernel, steps, shards),
            name="pack",
            out_shape=[half if step == shards - 1 else block for step in steps] + [half] * (shards - 1 in steps),
            in_specs=[ANY, ANY],
            out_specs=[VMEM] * (len(steps) + (shards - 1 in steps)),
            scratch_shapes=[
                pltpu.VMEM((len(steps), rows, columns), jnp.float32),
                pltpu.SemaphoreType.DMA((len(steps),)),
                pltpu.SemaphoreType.DMA((len(steps),)),
            ],
            compiler_params=pltpu.CompilerParams(vmem_limit_bytes=limit * 2**19),
            cost_estimate=pl.CostEstimate(
                flops=len(steps) * rows * columns, bytes_accessed=10 * len(steps) * rows * columns, transcendentals=0
            ),
        )(grad, mom)
    apart = payloads.pop()
    own = payloads.pop()
    blocks = [own, *(exchange(payload, step, shards) for step, payload in enumerate(payloads, 1))]
    late = exchange(apart, shards - 1, shards)
    (sums,) = pl.pallas_call(
        functools.partial(sums_kernel, shards),
        name="sums",
        out_shape=[table],
        in_specs=[VMEM] * (shards + 1),
        out_specs=[VMEM],
        compiler_params=pltpu.CompilerParams(vmem_limit_bytes=16 * 2**19),
        cost_estimate=pl.CostEstimate(flops=6 * grad.size, bytes_accessed=4 * grad.size, transcendentals=0),
    )(own, *payloads, apart)
    sums = lax.all_to_all(sums, ("grp", "shard"), 0, 0, tiled=True)
    side = shards * rows
    part = jax.ShapeDtypeStruct((rows, columns), jnp.bfloat16)
    cut = -(-rows // LANES) * LANES
    factors, x, gram = pl.pallas_call(
        functools.partial(begin_kernel, shards, element_count, cut),
        name="begin",
        out_shape=[
            jax.ShapeDtypeStruct((3, LANES), jnp.float32),
            jax.ShapeDtypeStruct((side - rows, columns), jnp.bfloat16),
            jax.ShapeDtypeStruct((side - rows, side - cut), jnp.bfloat16),
        ],
        in_specs=[VMEM] * shards,
        out_specs=[VMEM] * 3,
        compiler_params=pltpu.CompilerParams(vmem_limit_bytes=16 * 2**20),
        cost_estimate=pl.CostEstimate(flops=400_000_000, bytes_accessed=6 * grad.size, transcendentals=0),
    )(sums, blocks[1], blocks[0], *blocks[2:-1])
    first, blended, iterate = pl.pallas_call(
        functools.partial(newton_kernel, cut),
        name="newton",
        out_shape=[
            part,
            jax.ShapeDtypeStruct((side, side), jnp.bfloat16),
            jax.ShapeDtypeStruct((side, columns), jnp.bfloat16),
        ],
        in_specs=[VMEM] * 5,
        out_specs=[VMEM] * 3,
        compiler_params=pltpu.CompilerParams(vmem_limit_bytes=16 * 2**20),
        cost_estimate=pl.CostEstimate(flops=4_000_000_000, bytes_accessed=8 * grad.size, transcendentals=0),
    )(factors, blocks[-1], late, x, gram)
    returned = {1: exchange(first, 1, shards, back=True)}
    *others, = pl.pallas_call(
        apply_kernel,
        name="apply",
        out_shape=[part] * (shards - 1),
        in_specs=[VMEM] * 2,
        out_specs=[VMEM] * (shards - 1),
        compiler_params=pltpu.CompilerParams(vmem_limit_bytes=16 * 2**20),
        cost_estimate=pl.CostEstimate(flops=400_000_000, bytes_accessed=4 * grad.size, transcendentals=0),
    )(blended, iterate)
    left = [shards - 1, 0, *range(2, shards - 1)]
    for step, x in zip(left, others):
        returned[step] = exchange(x, step, shards, back=True) if step else x
    momentum_out, slot_rms = pl.pallas_call(
        functools.partial(momentum_kernel, shards),
        name="momentum",
        grid=(matrices,),
        out_shape=[
            jax.ShapeDtypeStruct(mom.shape, jnp.float32),
            jax.ShapeDtypeStruct((1, 1, CAP), jnp.float32),
        ],
        in_specs=[
            SMEM,
            pl.BlockSpec((3, LANES), lambda i: (0, 0)),
            pl.BlockSpec((devices, width), lambda i: (0, 0)),
            pl.BlockSpec((1, rows, columns), lambda i: (i, 0, 0)),
            pl.BlockSpec((1, rows, columns), lambda i: (i, 0, 0)),
        ],
        out_specs=[
            pl.BlockSpec((1, rows, columns), lambda i: (i, 0, 0)),
            pl.BlockSpec((1, 1, CAP), lambda i: (0, 0, 0)),
        ],
        compiler_params=pltpu.CompilerParams(vmem_limit_bytes=8 * 2**20),
        cost_estimate=pl.CostEstimate(flops=4 * grad.size, bytes_accessed=10 * grad.size, transcendentals=0),
    )(owner[0, :, 0], factors, sums, grad, mom)
    update = None
    for steps in (range(shards - 1), range(shards - 1, shards)):
        earlier = [] if update is None else [update]
        update = pl.pallas_call(
            functools.partial(place_kernel, steps, shards),
            name="place",
            out_shape=jax.ShapeDtypeStruct(grad.shape, jnp.bfloat16),
            in_specs=[VMEM] * len(steps) + [ANY] * len(earlier),
            out_specs=ANY,
            input_output_aliases={len(steps): 0} if earlier else {},
            scratch_shapes=[pltpu.SemaphoreType.DMA((shards,))],
            compiler_params=pltpu.CompilerParams(vmem_limit_bytes=8 * 2**20),
            cost_estimate=pl.CostEstimate(flops=0, bytes_accessed=len(steps) * grad.size, transcendentals=0),
        )(*(returned[step] for step in steps), *earlier)
    return (update[None], momentum_out[None], slot_rms)


def solution(mesh):
    return jax.shard_map(
        body,
        mesh=mesh,
        in_specs=(
            P("grp", None, "shard", None),
            P("grp", None, "shard", None),
            P("grp", None, None),
        ),
        out_specs=(
            P("grp", None, "shard", None),
            P("grp", None, "shard", None),
            P("grp", "shard", None),
        ),
        check_vma=False,
    )
```

```python
import functools
import math

import jax
import jax.numpy as jnp
from jax import lax
from jax.experimental import pallas as pl
from jax.experimental.pallas import tpu as pltpu
from jax.sharding import PartitionSpec as P


ITERS = 3
CAP = 2
LANES = 128
CHUNK = 24

QUINTIC_A = 3.4445
QUINTIC_B = -4.775
QUINTIC_C = 2.0315
MOMENTUM_DECAY = 0.95
CLIP_LEVEL = 0.5


VMEM = pl.BlockSpec(memory_space=pltpu.VMEM)
SMEM = pl.BlockSpec(memory_space=pltpu.SMEM)
ANY = pl.BlockSpec(memory_space=pl.ANY)


def mirrored(step, shards):
    bits = (shards - 1).bit_length() // 2
    if shards != 1 << (2 * bits):
        return step
    return step >> bits | (step & ((1 << bits) - 1)) << bits


def partner(group, me, place, shards):
    step = place % (shards - 1) + 1 if place else 0
    if shards & (shards - 1):
        return (me + step) % shards
    if isinstance(group, int):
        return me ^ (mirrored(step, shards) if group % 2 else step)
    return me ^ (step + (group & 1) * (mirrored(step, shards) - step))


def my_partner(place, shards):
    return partner(lax.axis_index("grp"), lax.axis_index("shard"), place, shards)


def exchange(block, step, shards, back=False):
    pairs = [
        (group * shards + i, group * shards + partner(group, i, step, shards))
        for group in range(lax.axis_size("grp"))
        for i in range(shards)
    ]
    return lax.ppermute(block, ("grp", "shard"), [(b, a) if back else (a, b) for a, b in pairs])


def pack_kernel(steps, shards, grad_hbm, mom_hbm, *rest):
    payloads, (mom_buf, grad_sem, mom_sem) = rest[: len(steps)], rest[-3:]
    rows = grad_hbm.shape[1]
    copies = []
    for at, step in enumerate(steps):
        target = my_partner(step, shards)
        into = payloads[at].at[pl.ds(0, rows)]
        grad_copy = pltpu.make_async_copy(grad_hbm.at[target], into, grad_sem.at[at])
        mom_copy = pltpu.make_async_copy(mom_hbm.at[target], mom_buf.at[at], mom_sem.at[at])
        mom_copy.start()
        grad_copy.start()
        copies.append((grad_copy, mom_copy))
    for at in range(len(steps)):
        copies[at][1].wait()
        payloads[at][pl.ds(rows, rows)] = mom_buf[at].astype(jnp.bfloat16)
    for grad_copy, _ in copies:
        grad_copy.wait()


def sums_kernel(shards, *rest):
    payloads, sums_ref = rest[:shards], rest[shards]
    rows = payloads[0].shape[0] // 2
    lane = lax.broadcasted_iota(jnp.int32, (1, sums_ref.shape[1]), 1)
    sums = jnp.zeros((1, sums_ref.shape[1]), jnp.float32)
    for step, payload in enumerate(payloads):
        totals = None
        for at in range(0, rows, CHUNK):
            grad = payload[pl.ds(at, CHUNK)].astype(jnp.float32)
            mom = payload[pl.ds(rows + at, CHUNK)].astype(jnp.float32)
            terms = [
                jnp.sum(p.reshape(CHUNK // 8, 8, p.shape[1]), axis=0)
                for p in (grad * grad, grad * mom, mom * mom)
            ]
            totals = terms if totals is None else [t + p for t, p in zip(totals, terms)]
        matrix = my_partner(step, shards)
        for kind, value in enumerate(totals):
            total = jnp.sum(jnp.sum(value, axis=0, keepdims=True), axis=1, keepdims=True)
            sums = jnp.where(lane == matrix + kind * shards, total, sums)
    sums_ref[...] = jnp.broadcast_to(sums, sums_ref.shape)


def lanes_sum(value, keep):
    return jnp.sum(jnp.where(keep, value, 0.0), axis=1, keepdims=True)


def coefficients(sums_ref, shards, element_count):
    sums = sums_ref[...]
    row = lax.broadcasted_iota(jnp.int32, sums.shape, 0)
    lane = lax.broadcasted_iota(jnp.int32, (1, sums.shape[1]), 1)
    first = lax.axis_index("grp") * shards
    every = jnp.sum(sums, axis=0, keepdims=True)
    group = jnp.sum(jnp.where((row >= first) & (row < first + shards), sums, 0.0), axis=0, keepdims=True)
    mean_square = lanes_sum(every, lane < shards) / element_count
    clip = jnp.minimum(jnp.float32(1.0), CLIP_LEVEL / jnp.sqrt(mean_square + 1e-06))
    gg, gm, mm = (lanes_sum(group, lane == lax.axis_index("shard") + kind * shards) for kind in range(3))
    alpha = clip * (1.0 + MOMENTUM_DECAY)
    beta = MOMENTUM_DECAY * MOMENTUM_DECAY
    square_sum = alpha * alpha * gg + (2.0 * beta) * alpha * gm + (beta * beta) * mm
    scale = 1.0 / (jnp.sqrt(jnp.maximum(square_sum, 0.0)) + 1e-07)
    return clip, alpha * scale, beta * scale


def iterate_rows(block, alpha, beta, rows):
    return (alpha * block[:rows].astype(jnp.float32) + beta * block[rows:].astype(jnp.float32)).astype(jnp.bfloat16)


def gram_of(left, right):
    return lax.dot_general(left, right, (((1,), (1,)), ((), ())), preferred_element_type=jnp.float32).astype(jnp.bfloat16)


def step_of(blended, iterate, first, rows, gain):
    at = pl.ds(first, rows)
    product = jnp.dot(blended[at], iterate[...], preferred_element_type=jnp.float32)
    return ((gain * QUINTIC_A) * iterate[at].astype(jnp.float32) + product).astype(jnp.bfloat16)


def begin_kernel(shards, element_count, cut, sums_ref, *rest):
    blocks, (factors_ref, x_ref, gram_ref) = rest[: shards - 1], rest[shards - 1 :]
    rows = blocks[0].shape[0] // 2
    factors = coefficients(sums_ref, shards, element_count)
    for at, factor in enumerate(factors):
        factors_ref[pl.ds(at, 1)] = jnp.broadcast_to(factor, (1, LANES))
    _, alpha, beta = (factor[0, 0] for factor in factors)
    for at, block in enumerate(blocks):
        x_ref[pl.ds(at * rows, rows)] = iterate_rows(block, alpha, beta, rows)
    gram_ref[...] = gram_of(x_ref[...], x_ref[cut - rows :])


def newton_kernel(cut, factors_ref, last_block, x_ref, gram_ref, early_ref, blended, iterate):
    rows, columns = early_ref.shape
    size = iterate.shape[0]
    iterate[pl.ds(0, rows)] = iterate_rows(last_block, factors_ref[1, 0], factors_ref[2, 0], rows)
    iterate[pl.ds(rows, size - rows)] = x_ref[...]
    for repeat in range(ITERS):
        last = repeat == ITERS - 1
        gain = math.sqrt(columns) if last else 1.0
        x = iterate[...]
        if repeat == 0:
            below = jnp.concatenate([gram_of(x[rows:], x[:cut]), gram_ref[...]], axis=1)
            gram = jnp.concatenate([gram_of(x[:rows], x), below], axis=0)
        else:
            gram = gram_of(x, x)
        squared = jnp.dot(gram, gram, preferred_element_type=jnp.float32)
        blended[...] = (
            (gain * QUINTIC_B) * gram.astype(jnp.float32) + (gain * QUINTIC_C) * squared
        ).astype(jnp.bfloat16)
        if last:
            early_ref[...] = step_of(blended, iterate, rows, rows, gain)
        else:
            iterate[...] = step_of(blended, iterate, 0, size, gain)


def apply_kernel(blended, iterate, *outs):
    rows, columns = outs[0].shape
    gain = math.sqrt(columns)
    outs[0][...] = step_of(blended, iterate, 0, rows, gain)
    x = step_of(blended, iterate, 2 * rows, (len(outs) - 1) * rows, gain)
    for at, out in enumerate(outs[1:]):
        out[...] = x[at * rows : (at + 1) * rows]


def place_kernel(steps, shards, *rest):
    blocks, out_hbm, sem = rest[: len(steps)], rest[-2], rest[-1]
    copies = []
    for step, block in zip(steps, blocks):
        copy = pltpu.make_async_copy(block, out_hbm.at[my_partner(step, shards)], sem.at[step])
        copy.start()
        copies.append(copy)
    for copy in copies:
        copy.wait()


def momentum_kernel(shards, owner_ref, factors_ref, sums_ref, grad_ref, mom_ref, out_ref, slot_ref):
    rows, columns = grad_ref.shape[1:]
    clip = factors_ref[0, 0]
    out_ref[...] = MOMENTUM_DECAY * mom_ref[...] + clip * grad_ref[...].astype(jnp.float32)

    @pl.when(pl.program_id(0) == 0)
    def _():
        me, group = lax.axis_index("shard"), lax.axis_index("grp")
        row = lax.broadcasted_iota(jnp.int32, sums_ref.shape, 0)
        inside = (row >= group * shards) & (row < (group + 1) * shards)
        sums = jnp.sum(jnp.where(inside, sums_ref[...], 0.0), axis=0, keepdims=True)
        lane = lax.broadcasted_iota(jnp.int32, sums.shape, 1)
        grad_part = clip * (1.0 + MOMENTUM_DECAY)
        mom_part = MOMENTUM_DECAY * MOMENTUM_DECAY
        slots = [jnp.float32(0.0)] * CAP
        count = jnp.int32(0)
        for matrix in range(shards):
            gg, gm, mm = (
                jnp.sum(jnp.where(lane == matrix + kind * shards, sums, 0.0)) for kind in range(3)
            )
            square = grad_part * grad_part * gg + 2.0 * grad_part * mom_part * gm + mom_part * mom_part * mm
            hit = owner_ref[matrix] == me
            for slot in range(CAP):
                slots[slot] = slots[slot] + jnp.where(hit & (count == slot), square, 0.0)
            count = count + hit.astype(jnp.int32)
        lane = lax.broadcasted_iota(jnp.int32, (1, CAP), 1)
        out = jnp.zeros((1, CAP), jnp.float32)
        for slot in range(CAP):
            out = jnp.where(lane == slot, slots[slot], out)
        slot_ref[...] = (jnp.sqrt(jnp.maximum(out, 0.0)) / math.sqrt(shards * rows * columns)).reshape(1, 1, CAP)


def body(gradient, momentum, owner):
    shards = lax.axis_size("shard")
    devices = shards * lax.axis_size("grp")
    matrices, rows, columns = gradient.shape[1:]
    assert matrices == shards
    element_count = matrices * rows * columns * devices
    width = -(-3 * matrices // LANES) * LANES
    grad, mom = gradient[0], momentum[0]
    block = jax.ShapeDtypeStruct((2 * rows, columns), jnp.bfloat16)
    table = jax.ShapeDtypeStruct((devices, width), jnp.float32)
    payloads = []
    for steps, limit in (([1], 106), ([2], 105), ([*range(3, shards), 0], 105)):
        payloads += pl.pallas_call(
            functools.partial(pack_kernel, steps, shards),
            name="pack",
            out_shape=[block] * len(steps),
            in_specs=[ANY, ANY],
            out_specs=[VMEM] * len(steps),
            scratch_shapes=[
                pltpu.VMEM((len(steps), rows, columns), jnp.float32),
                pltpu.SemaphoreType.DMA((len(steps),)),
                pltpu.SemaphoreType.DMA((len(steps),)),
            ],
            compiler_params=pltpu.CompilerParams(vmem_limit_bytes=limit * 2**19),
            cost_estimate=pl.CostEstimate(
                flops=len(steps) * rows * columns, bytes_accessed=10 * len(steps) * rows * columns, transcendentals=0
            ),
        )(grad, mom)
    own = payloads.pop()
    blocks = [own, *(exchange(payload, step, shards) for step, payload in enumerate(payloads[:-1], 1))]
    blocks.append(exchange(payloads[-1], shards - 1, shards))
    (sums,) = pl.pallas_call(
        functools.partial(sums_kernel, shards),
        name="sums",
        out_shape=[table],
        in_specs=[VMEM] * shards,
        out_specs=[VMEM],
        compiler_params=pltpu.CompilerParams(vmem_limit_bytes=16 * 2**19),
        cost_estimate=pl.CostEstimate(flops=6 * grad.size, bytes_accessed=4 * grad.size, transcendentals=0),
    )(own, *payloads)
    sums = lax.all_to_all(sums, ("grp", "shard"), 0, 0, tiled=True)
    side = shards * rows
    part = jax.ShapeDtypeStruct((rows, columns), jnp.bfloat16)
    cut = -(-rows // LANES) * LANES
    factors, x, gram = pl.pallas_call(
        functools.partial(begin_kernel, shards, element_count, cut),
        name="begin",
        out_shape=[
            jax.ShapeDtypeStruct((3, LANES), jnp.float32),
            jax.ShapeDtypeStruct((side - rows, columns), jnp.bfloat16),
            jax.ShapeDtypeStruct((side - rows, side - cut), jnp.bfloat16),
        ],
        in_specs=[VMEM] * shards,
        out_specs=[VMEM] * 3,
        compiler_params=pltpu.CompilerParams(vmem_limit_bytes=16 * 2**20),
        cost_estimate=pl.CostEstimate(flops=400_000_000, bytes_accessed=6 * grad.size, transcendentals=0),
    )(sums, blocks[1], blocks[0], *blocks[2:-1])
    first, blended, iterate = pl.pallas_call(
        functools.partial(newton_kernel, cut),
        name="newton",
        out_shape=[
            part,
            jax.ShapeDtypeStruct((side, side), jnp.bfloat16),
            jax.ShapeDtypeStruct((side, columns), jnp.bfloat16),
        ],
        in_specs=[VMEM] * 4,
        out_specs=[VMEM] * 3,
        compiler_params=pltpu.CompilerParams(vmem_limit_bytes=16 * 2**20),
        cost_estimate=pl.CostEstimate(flops=4_000_000_000, bytes_accessed=8 * grad.size, transcendentals=0),
    )(factors, blocks[-1], x, gram)
    returned = {1: exchange(first, 1, shards, back=True)}
    *others, = pl.pallas_call(
        apply_kernel,
        name="apply",
        out_shape=[part] * (shards - 1),
        in_specs=[VMEM] * 2,
        out_specs=[VMEM] * (shards - 1),
        compiler_params=pltpu.CompilerParams(vmem_limit_bytes=16 * 2**20),
        cost_estimate=pl.CostEstimate(flops=400_000_000, bytes_accessed=4 * grad.size, transcendentals=0),
    )(blended, iterate)
    left = [shards - 1, 0, *range(2, shards - 1)]
    for step, x in zip(left, others):
        returned[step] = exchange(x, step, shards, back=True) if step else x
    momentum_out, slot_rms = pl.pallas_call(
        functools.partial(momentum_kernel, shards),
        name="momentum",
        grid=(matrices,),
        out_shape=[
            jax.ShapeDtypeStruct(mom.shape, jnp.float32),
            jax.ShapeDtypeStruct((1, 1, CAP), jnp.float32),
        ],
        in_specs=[
            SMEM,
            pl.BlockSpec((3, LANES), lambda i: (0, 0)),
            pl.BlockSpec((devices, width), lambda i: (0, 0)),
            pl.BlockSpec((1, rows, columns), lambda i: (i, 0, 0)),
            pl.BlockSpec((1, rows, columns), lambda i: (i, 0, 0)),
        ],
        out_specs=[
            pl.BlockSpec((1, rows, columns), lambda i: (i, 0, 0)),
            pl.BlockSpec((1, 1, CAP), lambda i: (0, 0, 0)),
        ],
        compiler_params=pltpu.CompilerParams(vmem_limit_bytes=8 * 2**20),
        cost_estimate=pl.CostEstimate(flops=4 * grad.size, bytes_accessed=10 * grad.size, transcendentals=0),
    )(owner[0, :, 0], factors, sums, grad, mom)
    update = None
    for steps in (range(shards - 1), range(shards - 1, shards)):
        earlier = [] if update is None else [update]
        update = pl.pallas_call(
            functools.partial(place_kernel, steps, shards),
            name="place",
            out_shape=jax.ShapeDtypeStruct(grad.shape, jnp.bfloat16),
            in_specs=[VMEM] * len(steps) + [ANY] * len(earlier),
            out_specs=ANY,
            input_output_aliases={len(steps): 0} if earlier else {},
            scratch_shapes=[pltpu.SemaphoreType.DMA((shards,))],
            compiler_params=pltpu.CompilerParams(vmem_limit_bytes=8 * 2**20),
            cost_estimate=pl.CostEstimate(flops=0, bytes_accessed=len(steps) * grad.size, transcendentals=0),
        )(*(returned[step] for step in steps), *earlier)
    return (update[None], momentum_out[None], slot_rms)


def solution(mesh):
    return jax.shard_map(
        body,
        mesh=mesh,
        in_specs=(
            P("grp", None, "shard", None),
            P("grp", None, "shard", None),
            P("grp", None, None),
        ),
        out_specs=(
            P("grp", None, "shard", None),
            P("grp", None, "shard", None),
            P("grp", "shard", None),
        ),
        check_vma=False,
    )
```
